512 devices in a mesh: tmpl: 16 (over y, x_hi, core), seg: 32 (over x_lo, z).
Axes of the slice: x: 4 (x_hi: 2, x_lo: 2; x = x_hi * 2 + x_lo), y: 4, z: 16, core: 2. Of those that a mesh axis runs over, the one named last changes fastest.
Arguments:
- strain: bfloat16 [32, 2, 512, 512], P('seg'), may hold values from -6 to 6
- bank: bfloat16 [512, 2, 512, 512], P(('tmpl', 'seg'))
- owners: int32 [16, 2], P('tmpl'), may hold values from 0 to 31, as said below
- gate_start: int32 [32, 4], P('seg'), may hold values from 0 to 258047
- gate_width: int32 [32, 4], P('seg'), may hold values from 1 to 4096
Outputs:
- network: bfloat16 [32, 32, 131072], P('tmpl', 'seg')
- loudest: bfloat16 [32, 131072], P('seg')
The draws below stay inside these ranges and needn't reach their ends.
Inputs may be any that keep to these rules, and one draw needn't show every extreme that they name: `owners`: within each row the 2 entries are distinct.
All inputs are finite; a program needn't handle non-finite values.
Results may differ from the reference program's by a relative error of at most 0.0051.
Values may be sent and summed in bfloat16 or wider, within the bound.
No kernel may reach another device: no remote copies, remote signals or barrier semaphores. Data moves between devices by JAX's collectives and lax.ppermute only.
A program may use at most 64 MiB of HBM per device.

```python
import math
import jax
import jax.numpy as jnp
from jax import lax

N1 = 512
N2 = 512
STEPS = 2
GATES = 4
GMAX = 4096
TEMPLATES = 32
N_TMPL = 16
N_SEG = 32


def draw_bank(key, part):
    key_base, key_rows = jax.random.split(key, 2)
    shape = (N_TMPL * N_SEG, 2, N1, N2)
    base = jax.random.normal(key_base, shape, jnp.float32)
    row_scale = jnp.exp(jax.random.uniform(key_rows, (N_TMPL * N_SEG, 1, N1, 1), jnp.float32) * math.log(10.0))
    return (base * row_scale).astype(jnp.bfloat16)


def draw_owners(key, part):
    row_keys = jax.random.split(key, N_TMPL)
    return jax.vmap(lambda row_key: jax.random.permutation(row_key, N_SEG)[:STEPS])(row_keys).astype(jnp.int32)


def touch_ends(result, own_key, smallest, high):
    extent = result.shape
    spot = [jax.random.randint(jax.random.fold_in(own_key, axis), (), 0, extent[axis]) for axis in range(len(extent))]
    result = result.at[tuple(spot)].set(smallest)
    longest = extent.index(max(extent))
    spot[longest] = (spot[longest] + 1) % extent[longest]
    return result.at[tuple(spot)].set(high)


def level_of(rng, shape, pieces, low, top_value):
    def one(axis_at, shards_of):
        heights = jax.random.uniform(jax.random.fold_in(jax.random.fold_in(rng, 6), axis_at), (shards_of,), jnp.float32, low / len(pieces), top_value / len(pieces))
        return jnp.repeat(jnp.exp(heights), shape[axis_at] // shards_of).reshape((-1,) + (1,) * (len(shape) - axis_at - 1))

    level = one(*pieces[0])
    for cut in pieces[1:]:
        level = level * one(*cut)
    return level


def centred(stream_key, dims, scale, bound, pieces=(), kind=jnp.bfloat16):
    result = jax.random.normal(stream_key, dims, jnp.float32) * scale
    if len(pieces) > 0:
        result = level_of(stream_key, dims, pieces, -0.22, 0.18) * result
    return jnp.clip(result, min=-bound, max=bound).astype(kind)


def setup_inputs(seed: int = 0) -> dict:
    arg_keys = jax.random.split(jax.random.key(seed), 6)
    strain = centred(arg_keys[0], (N_SEG, 2, N1, N2), 1.0, 6.0, ((0, 32),))
    bank = draw_bank(jax.random.fold_in(arg_keys[5], 71), 0)
    owners = draw_owners(jax.random.fold_in(arg_keys[5], 71), 0)
    gate_start = touch_ends(jax.random.randint(arg_keys[3], (N_SEG, GATES), 0, N1 * N2 - GMAX), jax.random.fold_in(arg_keys[3], 1), 0, (N1 * N2 - GMAX) - 1).astype(jnp.int32)
    gate_width = touch_ends(jax.random.randint(arg_keys[4], (N_SEG, GATES), 1, GMAX + 1), jax.random.fold_in(arg_keys[4], 1), 1, GMAX).astype(jnp.int32)
    return {"strain": strain, "bank": bank, "owners": owners, "gate_start": gate_start, "gate_width": gate_width}


def dft_table(length):
    positions = jnp.arange(length, dtype=jnp.int32)
    angles = (positions[:, None] * positions[None, :] % length).astype(jnp.float32) * (2.0 * math.pi / length)
    return jnp.concatenate([jnp.cos(angles), jnp.sin(angles)], axis=0).astype(jnp.bfloat16)

def twiddle(row_count, col_count):
    row_index = jnp.arange(row_count, dtype=jnp.int32)[:, None]
    col_index = jnp.arange(col_count, dtype=jnp.int32)[None, :]
    angles = (row_index * col_index % (row_count * col_count)).astype(jnp.float32) * (2.0 * math.pi / (row_count * col_count))
    return (jnp.cos(angles), jnp.sin(angles))

def gate_mask(starts, widths, row_count, col_count):
    moment = jnp.arange(row_count, dtype=jnp.int32)[:, None] * col_count + jnp.arange(col_count, dtype=jnp.int32)[None, :]
    flags = jnp.zeros((row_count, col_count), dtype=jnp.bool_)
    for number in range(starts.shape[0]):
        flags = flags | (moment >= starts[number]) & (moment < starts[number] + widths[number])
    return flags

def filter_power(template, series, flags, first_table, second_table, twiddle_cos, twiddle_sin):
    count_a = template.shape[1]
    count_b = template.shape[2]
    out_rows = second_table.shape[0] // 2
    tmpl_re = template[0].astype(jnp.float32)
    tmpl_im = template[1].astype(jnp.float32)
    data_re = series[0].astype(jnp.float32)
    data_im = series[1].astype(jnp.float32)
    prod_re = data_re * tmpl_re + data_im * tmpl_im
    prod_im = data_im * tmpl_re - data_re * tmpl_im
    joined = jnp.concatenate([prod_re, prod_im], axis=1).astype(jnp.bfloat16)
    section_one = jnp.dot(first_table, joined, preferred_element_type=jnp.float32)
    section_re = section_one[:count_a, :count_b] - section_one[count_a:, count_b:]
    section_im = section_one[:count_a, count_b:] + section_one[count_a:, :count_b]
    turned = jnp.concatenate([section_re * twiddle_cos - section_im * twiddle_sin, section_re * twiddle_sin + section_im * twiddle_cos], axis=0).astype(jnp.bfloat16)
    section_two = lax.dot_general(second_table, turned, (((1,), (1,)), ((), ())), preferred_element_type=jnp.float32)
    snr_re = section_two[:out_rows, :count_a] - section_two[out_rows:, count_a:]
    snr_im = section_two[:out_rows, count_a:] + section_two[out_rows:, :count_a]
    norm_sq = jnp.sum(tmpl_re * tmpl_re + tmpl_im * tmpl_im) + 1e-06
    snr_power = (snr_re * snr_re + snr_im * snr_im) / norm_sq
    return jnp.where(flags, 0.0, snr_power).astype(jnp.bfloat16)

def reference(strain, bank, owners, gate_start, gate_width):
    first_table = dft_table(N1)
    second_table = dft_table(N2)
    twiddle_cos, twiddle_sin = twiddle(N1, N2)
    gate_masks = jax.vmap(lambda starts, widths: gate_mask(starts, widths, N2, N1))(gate_start, gate_width)
    chosen_rows = (jnp.arange(N_TMPL, dtype=jnp.int32)[:, None] * N_SEG + owners).reshape(-1)
    chosen = bank[chosen_rows]

    def per_template(template):
        return lax.map(lambda inputs: filter_power(template, inputs[0], inputs[1], first_table, second_table, twiddle_cos, twiddle_sin), (strain, gate_masks))
    powers = lax.map(per_template, chosen)
    paired = powers.reshape(TEMPLATES, N_SEG // 2, 2, 2, N2 // 2, N1).astype(jnp.float32)
    summed = paired + paired[:, :, ::-1]
    network = jnp.stack([summed[:, :, 0, 0], summed[:, :, 1, 1]], axis=2)
    network = jnp.sqrt(network).astype(jnp.bfloat16).reshape(TEMPLATES, N_SEG, N2 // 2 * N1)
    loudest = lax.optimization_barrier(jnp.max(network, axis=0))
    return (network, loudest)
```

```python
import math

import jax
import jax.numpy as jnp
from jax import lax
from jax.sharding import PartitionSpec as P


def spread(blocks, axis, holders):
    count = lax.axis_size(axis)
    rounds = [count // 2]
    apart = 1
    while apart < count // 2:
        rounds.append(apart)
        apart *= 2
    mine = lax.axis_index(axis)
    picked = [
        jnp.where(mine == holders[number], block, jnp.zeros_like(block))
        for number, block in enumerate(blocks)
    ]
    shape = picked[0].shape
    flat = jnp.stack(picked).reshape(-1, shape[-1])
    for apart in rounds:
        half = flat.shape[0] // 2
        side = (mine // apart) % 2
        keep = lax.dynamic_slice_in_dim(flat, side * half, half, 0)
        send = lax.dynamic_slice_in_dim(flat, (1 - side) * half, half, 0)
        route = [(low, low ^ apart) for low in range(count)]
        flat = keep + lax.ppermute(send, axis, route)
    for apart in reversed(rounds):
        side = (mine // apart) % 2
        route = [(low, low ^ apart) for low in range(count)]
        other = lax.ppermute(flat, axis, route)
        flat = jnp.where(
            side == 0,
            jnp.concatenate([flat, other], axis=0),
            jnp.concatenate([other, flat], axis=0),
        )
    return flat.reshape((len(blocks),) + shape)


def butterfly_max(block, axis):
    count = lax.axis_size(axis)
    apart = count // 2
    while apart >= 1:
        route = [(low, low ^ apart) for low in range(count)]
        block = jnp.maximum(block, lax.ppermute(block, axis, route))
        apart //= 2
    return block


def from_partner(block, axis, apart):
    count = lax.axis_size(axis)
    route = []
    for low in range(count):
        high = low | 1 << apart
        if high != low and high < count:
            route += [(low, high), (high, low)]
    return lax.ppermute(block, axis, route)


def dft_table(length):
    positions = jnp.arange(length, dtype=jnp.int32)
    angles = (positions[:, None] * positions[None, :] % length).astype(jnp.float32) * (
        2.0 * math.pi / length
    )
    return jnp.concatenate([jnp.cos(angles), jnp.sin(angles)], axis=0).astype(jnp.bfloat16)


def twiddle(row_count, col_count):
    row_index = jnp.arange(row_count, dtype=jnp.int32)[:, None]
    col_index = jnp.arange(col_count, dtype=jnp.int32)[None, :]
    angles = (row_index * col_index % (row_count * col_count)).astype(jnp.float32) * (
        2.0 * math.pi / (row_count * col_count)
    )
    return (jnp.cos(angles), jnp.sin(angles))


def gate_mask(starts, widths, row_count, col_count):
    moment = (
        jnp.arange(row_count, dtype=jnp.int32)[:, None] * col_count
        + jnp.arange(col_count, dtype=jnp.int32)[None, :]
    )
    flags = jnp.zeros((row_count, col_count), dtype=jnp.bool_)
    for number in range(starts.shape[0]):
        flags = flags | (moment >= starts[number]) & (moment < starts[number] + widths[number])
    return flags


def filter_power(template, series, flags, first_table, second_table, twiddle_cos, twiddle_sin):
    count_a = template.shape[1]
    count_b = template.shape[2]
    out_rows = second_table.shape[0] // 2
    tmpl_re = template[0].astype(jnp.float32)
    tmpl_im = template[1].astype(jnp.float32)
    data_re = series[0].astype(jnp.float32)
    data_im = series[1].astype(jnp.float32)
    prod_re = data_re * tmpl_re + data_im * tmpl_im
    prod_im = data_im * tmpl_re - data_re * tmpl_im
    joined = jnp.concatenate([prod_re, prod_im], axis=1).astype(jnp.bfloat16)
    section_one = jnp.dot(first_table, joined, preferred_element_type=jnp.float32)
    section_re = section_one[:count_a, :count_b] - section_one[count_a:, count_b:]
    section_im = section_one[:count_a, count_b:] + section_one[count_a:, :count_b]
    turned = jnp.concatenate(
        [
            section_re * twiddle_cos - section_im * twiddle_sin,
            section_re * twiddle_sin + section_im * twiddle_cos,
        ],
        axis=0,
    ).astype(jnp.bfloat16)
    section_two = lax.dot_general(
        second_table, turned, (((1,), (1,)), ((), ())), preferred_element_type=jnp.float32
    )
    snr_re = section_two[:out_rows, :count_a] - section_two[out_rows:, count_a:]
    snr_im = section_two[:out_rows, count_a:] + section_two[out_rows:, :count_a]
    norm_sq = jnp.sum(tmpl_re * tmpl_re + tmpl_im * tmpl_im) + 1e-06
    snr_power = (snr_re * snr_re + snr_im * snr_im) / norm_sq
    return jnp.where(flags, 0.0, snr_power).astype(jnp.bfloat16)


def per_device(strain, bank, owners, gate_start, gate_width):
    count_a = strain.shape[2]
    count_b = strain.shape[3]
    block_count = owners.shape[1]
    half_rows = count_b // 2
    first_table = dft_table(count_a)
    second_table = dft_table(count_b)
    twiddle_cos, twiddle_sin = twiddle(count_a, count_b)
    flags = gate_mask(gate_start[0], gate_width[0], count_b, count_a)
    series = strain[0]
    stored = bank[0]
    detector_side = lax.axis_index("seg") % 2
    row_start = detector_side * half_rows
    templates = spread([stored] * block_count, "seg", [owners[0, n] for n in range(block_count)])
    results = []
    for number in range(block_count):
        results.append(
            filter_power(
                templates[number],
                series,
                flags,
                first_table,
                second_table,
                twiddle_cos,
                twiddle_sin,
            )
        )
    stacked = jnp.stack(results)
    own_half = lax.dynamic_slice_in_dim(stacked, row_start, half_rows, 1)
    other_half = lax.dynamic_slice_in_dim(stacked, half_rows - row_start, half_rows, 1)
    partner = from_partner(other_half, "seg", 0)
    network = jnp.sqrt(own_half.astype(jnp.float32) + partner.astype(jnp.float32)).astype(
        jnp.bfloat16
    )
    loudest = butterfly_max(jnp.max(network, axis=0), "tmpl")
    network = network.reshape(block_count, 1, half_rows * count_a)
    loudest = loudest.reshape(1, half_rows * count_a)
    return (network, loudest)


def solution(mesh):
    in_specs = (
        P("seg", None, None, None),
        P(("tmpl", "seg"), None, None, None),
        P("tmpl", None),
        P("seg", None),
        P("seg", None),
    )
    out_specs = (P("tmpl", "seg", None), P("seg", None))
    return jax.shard_map(
        per_device, mesh=mesh, in_specs=in_specs, out_specs=out_specs, check_vma=False
    )
```

```python
import math

import jax
import jax.numpy as jnp
from jax import lax
from jax.sharding import PartitionSpec as P


def spread(blocks, axis, holders):
    count = lax.axis_size(axis)
    rounds = [count // 2]
    apart = 1
    while apart < count // 2:
        rounds.append(apart)
        apart *= 2
    mine = lax.axis_index(axis)
    picked = [
        jnp.where(mine == holders[number], block, jnp.zeros_like(block))
        for number, block in enumerate(blocks)
    ]
    shape = picked[0].shape
    flat = jnp.stack(picked).reshape(-1, shape[-1])
    for apart in rounds:
        half = flat.shape[0] // 2
        side = (mine // apart) % 2
        keep = lax.dynamic_slice_in_dim(flat, side * half, half, 0)
        send = lax.dynamic_slice_in_dim(flat, (1 - side) * half, half, 0)
        route = [(low, low ^ apart) for low in range(count)]
        flat = keep + lax.ppermute(send, axis, route)
    for apart in reversed(rounds[1:]):
        side = (mine // apart) % 2
        route = [(low, low ^ apart) for low in range(count)]
        other = lax.ppermute(flat, axis, route)
        flat = jnp.where(
            side == 0,
            jnp.concatenate([flat, other], axis=0),
            jnp.concatenate([other, flat], axis=0),
        )
    route = [(low, low ^ rounds[0]) for low in range(count)]
    other = lax.ppermute(flat, axis, route)
    side = (mine // rounds[0]) % 2
    return flat.reshape(shape), other.reshape(shape), side


def butterfly_max(block, axis):
    count = lax.axis_size(axis)
    apart = count // 2
    while apart >= 1:
        route = [(low, low ^ apart) for low in range(count)]
        block = jnp.maximum(block, lax.ppermute(block, axis, route))
        apart //= 2
    return block


def from_partner(block, axis, apart):
    count = lax.axis_size(axis)
    route = []
    for low in range(count):
        high = low | 1 << apart
        if high != low and high < count:
            route += [(low, high), (high, low)]
    return lax.ppermute(block, axis, route)


def dft_table(length):
    positions = jnp.arange(length, dtype=jnp.int32)
    angles = (positions[:, None] * positions[None, :] % length).astype(jnp.float32) * (
        2.0 * math.pi / length
    )
    return jnp.concatenate([jnp.cos(angles), jnp.sin(angles)], axis=0).astype(jnp.bfloat16)


def twiddle(row_count, col_count):
    row_index = jnp.arange(row_count, dtype=jnp.int32)[:, None]
    col_index = jnp.arange(col_count, dtype=jnp.int32)[None, :]
    angles = (row_index * col_index % (row_count * col_count)).astype(jnp.float32) * (
        2.0 * math.pi / (row_count * col_count)
    )
    return (jnp.cos(angles), jnp.sin(angles))


def gate_mask(starts, widths, row_count, col_count):
    moment = (
        jnp.arange(row_count, dtype=jnp.int32)[:, None] * col_count
        + jnp.arange(col_count, dtype=jnp.int32)[None, :]
    )
    flags = jnp.zeros((row_count, col_count), dtype=jnp.bool_)
    for number in range(starts.shape[0]):
        flags = flags | (moment >= starts[number]) & (moment < starts[number] + widths[number])
    return flags


def filter_power(template, series, flags, first_table, second_table, twiddle_cos, twiddle_sin):
    count_a = template.shape[1]
    count_b = template.shape[2]
    out_rows = second_table.shape[0] // 2
    tmpl_re = template[0].astype(jnp.float32)
    tmpl_im = template[1].astype(jnp.float32)
    data_re = series[0].astype(jnp.float32)
    data_im = series[1].astype(jnp.float32)
    prod_re = data_re * tmpl_re + data_im * tmpl_im
    prod_im = data_im * tmpl_re - data_re * tmpl_im
    joined = jnp.concatenate([prod_re, prod_im], axis=1).astype(jnp.bfloat16)
    section_one = jnp.dot(first_table, joined, preferred_element_type=jnp.float32)
    section_re = section_one[:count_a, :count_b] - section_one[count_a:, count_b:]
    section_im = section_one[:count_a, count_b:] + section_one[count_a:, :count_b]
    turned = jnp.concatenate(
        [
            section_re * twiddle_cos - section_im * twiddle_sin,
            section_re * twiddle_sin + section_im * twiddle_cos,
        ],
        axis=0,
    ).astype(jnp.bfloat16)
    section_two = lax.dot_general(
        second_table, turned, (((1,), (1,)), ((), ())), preferred_element_type=jnp.float32
    )
    snr_re = section_two[:out_rows, :count_a] - section_two[out_rows:, count_a:]
    snr_im = section_two[:out_rows, count_a:] + section_two[out_rows:, :count_a]
    norm_sq = jnp.sum(tmpl_re * tmpl_re + tmpl_im * tmpl_im) + 1e-06
    snr_power = (snr_re * snr_re + snr_im * snr_im) / norm_sq
    return jnp.where(flags, 0.0, snr_power).astype(jnp.bfloat16)


def per_device(strain, bank, owners, gate_start, gate_width):
    count_a = strain.shape[2]
    count_b = strain.shape[3]
    block_count = owners.shape[1]
    half_rows = count_b // 2
    first_table = dft_table(count_a)
    second_table = dft_table(count_b)
    twiddle_cos, twiddle_sin = twiddle(count_a, count_b)
    flags = gate_mask(gate_start[0], gate_width[0], count_b, count_a)
    series = strain[0]
    stored = bank[0]
    detector_side = lax.axis_index("seg") % 2
    row_start = detector_side * half_rows
    own_tmpl, other_tmpl, side = spread(
        [stored] * block_count, "seg", [owners[0, n] for n in range(block_count)]
    )
    networks = []
    power = None
    for template in (own_tmpl, other_tmpl):
        if power is not None:
            template, power = lax.optimization_barrier((template, power))
        power = filter_power(
            template, series, flags, first_table, second_table, twiddle_cos, twiddle_sin
        )
        own_half = lax.dynamic_slice_in_dim(power, row_start, half_rows, 0)
        other_half = lax.dynamic_slice_in_dim(power, half_rows - row_start, half_rows, 0)
        partner = from_partner(other_half, "seg", 0)
        networks.append(
            jnp.sqrt(own_half.astype(jnp.float32) + partner.astype(jnp.float32)).astype(
                jnp.bfloat16
            )
        )
    loudest = butterfly_max(jnp.maximum(networks[0], networks[1]), "tmpl")
    network = jnp.where(
        side == 0, jnp.stack([networks[0], networks[1]]), jnp.stack([networks[1], networks[0]])
    )
    network = network.reshape(block_count, 1, half_rows * count_a)
    loudest = loudest.reshape(1, half_rows * count_a)
    return (network, loudest)


def solution(mesh):
    in_specs = (
        P("seg", None, None, None),
        P(("tmpl", "seg"), None, None, None),
        P("tmpl", None),
        P("seg", None),
        P("seg", None),
    )
    out_specs = (P("tmpl", "seg", None), P("seg", None))
    return jax.shard_map(
        per_device, mesh=mesh, in_specs=in_specs, out_specs=out_specs, check_vma=False
    )
```

```python
import math

import jax
import jax.numpy as jnp
from jax import lax
from jax.sharding import PartitionSpec as P


def spread(blocks, axis, holders):
    count = lax.axis_size(axis)
    rounds = [count // 2]
    apart = 1
    while apart < count // 2:
        rounds.append(apart)
        apart *= 2
    mine = lax.axis_index(axis)
    picked = [
        jnp.where(mine == holders[number], block, jnp.zeros_like(block))
        for number, block in enumerate(blocks)
    ]
    shape = picked[0].shape
    flat = jnp.stack(picked).reshape(-1, shape[-1])
    for apart in rounds:
        half = flat.shape[0] // 2
        side = (mine // apart) % 2
        keep = lax.dynamic_slice_in_dim(flat, side * half, half, 0)
        send = lax.dynamic_slice_in_dim(flat, (1 - side) * half, half, 0)
        route = [(low, low ^ apart) for low in range(count)]
        flat = keep + lax.ppermute(send, axis, route)
    for apart in reversed(rounds[1:]):
        side = (mine // apart) % 2
        route = [(low, low ^ apart) for low in range(count)]
        other = lax.ppermute(flat, axis, route)
        flat = jnp.where(
            side == 0,
            jnp.concatenate([flat, other], axis=0),
            jnp.concatenate([other, flat], axis=0),
        )
    route = [(low, low ^ rounds[0]) for low in range(count)]
    other = lax.ppermute(flat, axis, route)
    side = (mine // rounds[0]) % 2
    return flat.reshape(shape), other.reshape(shape), side


def butterfly_max(block, axis):
    count = lax.axis_size(axis)
    apart = count // 2
    while apart >= 1:
        route = [(low, low ^ apart) for low in range(count)]
        block = jnp.maximum(block, lax.ppermute(block, axis, route))
        apart //= 2
    return block


def from_partner(block, axis, apart):
    count = lax.axis_size(axis)
    route = []
    for low in range(count):
        high = low | 1 << apart
        if high != low and high < count:
            route += [(low, high), (high, low)]
    return lax.ppermute(block, axis, route)


def dft_table(length):
    positions = jnp.arange(length, dtype=jnp.int32)
    angles = (positions[:, None] * positions[None, :] % length).astype(jnp.float32) * (
        2.0 * math.pi / length
    )
    return jnp.concatenate([jnp.cos(angles), jnp.sin(angles)], axis=0).astype(jnp.bfloat16)


def twiddle(row_count, col_count):
    row_index = jnp.arange(row_count, dtype=jnp.int32)[:, None]
    col_index = jnp.arange(col_count, dtype=jnp.int32)[None, :]
    angles = (row_index * col_index % (row_count * col_count)).astype(jnp.float32) * (
        2.0 * math.pi / (row_count * col_count)
    )
    return (jnp.cos(angles), jnp.sin(angles))


def gate_mask(starts, widths, row_count, col_count):
    moment = (
        jnp.arange(row_count, dtype=jnp.int32)[:, None] * col_count
        + jnp.arange(col_count, dtype=jnp.int32)[None, :]
    )
    flags = jnp.zeros((row_count, col_count), dtype=jnp.bool_)
    for number in range(starts.shape[0]):
        flags = flags | (moment >= starts[number]) & (moment < starts[number] + widths[number])
    return flags


def filter_power(template, series, flags, first_table, second_table, twiddle_cos, twiddle_sin):
    count_a = template.shape[1]
    count_b = template.shape[2]
    out_rows = second_table.shape[0] // 2
    tmpl_re = template[0].astype(jnp.float32)
    tmpl_im = template[1].astype(jnp.float32)
    data_re = series[0].astype(jnp.float32)
    data_im = series[1].astype(jnp.float32)
    prod_re = data_re * tmpl_re + data_im * tmpl_im
    prod_im = data_im * tmpl_re - data_re * tmpl_im
    joined = jnp.concatenate([prod_re, prod_im], axis=1).astype(jnp.bfloat16)
    section_one = jnp.dot(first_table, joined, preferred_element_type=jnp.float32)
    section_re = section_one[:count_a, :count_b] - section_one[count_a:, count_b:]
    section_im = section_one[:count_a, count_b:] + section_one[count_a:, :count_b]
    turned = jnp.concatenate(
        [
            section_re * twiddle_cos - section_im * twiddle_sin,
            section_re * twiddle_sin + section_im * twiddle_cos,
        ],
        axis=0,
    ).astype(jnp.bfloat16)
    section_two = lax.dot_general(
        second_table, turned, (((1,), (1,)), ((), ())), preferred_element_type=jnp.float32
    )
    snr_re = section_two[:out_rows, :count_a] - section_two[out_rows:, count_a:]
    snr_im = section_two[:out_rows, count_a:] + section_two[out_rows:, :count_a]
    norm_sq = jnp.sum(tmpl_re * tmpl_re + tmpl_im * tmpl_im) + 1e-06
    snr_power = (snr_re * snr_re + snr_im * snr_im) / norm_sq
    return jnp.where(flags, 0.0, snr_power).astype(jnp.bfloat16)


def per_device(strain, bank, owners, gate_start, gate_width):
    count_a = strain.shape[2]
    count_b = strain.shape[3]
    block_count = owners.shape[1]
    half_rows = count_b // 2
    first_table = dft_table(count_a)
    second_table = dft_table(count_b)
    twiddle_cos, twiddle_sin = twiddle(count_a, count_b)
    flags = gate_mask(gate_start[0], gate_width[0], count_b, count_a)
    first_table, second_table, twiddle_cos, twiddle_sin, flags = lax.optimization_barrier(
        (first_table, second_table, twiddle_cos, twiddle_sin, flags)
    )
    series = strain[0]
    stored = bank[0]
    detector_side = lax.axis_index("seg") % 2
    row_start = detector_side * half_rows
    own_tmpl, other_tmpl, side = spread(
        [stored] * block_count, "seg", [owners[0, n] for n in range(block_count)]
    )
    networks = []
    power = None
    for template in (own_tmpl, other_tmpl):
        if power is not None:
            template, power = lax.optimization_barrier((template, power))
        power = filter_power(
            template, series, flags, first_table, second_table, twiddle_cos, twiddle_sin
        )
        own_half = lax.dynamic_slice_in_dim(power, row_start, half_rows, 0)
        other_half = lax.dynamic_slice_in_dim(power, half_rows - row_start, half_rows, 0)
        partner = from_partner(other_half, "seg", 0)
        networks.append(
            jnp.sqrt(own_half.astype(jnp.float32) + partner.astype(jnp.float32)).astype(
                jnp.bfloat16
            )
        )
    loudest = butterfly_max(jnp.maximum(networks[0], networks[1]), "tmpl")
    network = jnp.where(
        side == 0, jnp.stack([networks[0], networks[1]]), jnp.stack([networks[1], networks[0]])
    )
    network = network.reshape(block_count, 1, half_rows * count_a)
    loudest = loudest.reshape(1, half_rows * count_a)
    return (network, loudest)


def solution(mesh):
    in_specs = (
        P("seg", None, None, None),
        P(("tmpl", "seg"), None, None, None),
        P("tmpl", None),
        P("seg", None),
        P("seg", None),
    )
    out_specs = (P("tmpl", "seg", None), P("seg", None))
    return jax.shard_map(
        per_device, mesh=mesh, in_specs=in_specs, out_specs=out_specs, check_vma=False
    )
```

```python
import math

import jax
import jax.numpy as jnp
from jax import lax
from jax.sharding import Mesh
from jax.sharding import PartitionSpec as P


def spread(stored, owners, row_axis, ring_axis):
    ring = lax.axis_size(ring_axis)
    row = lax.axis_index(row_axis)
    spot = lax.axis_index(ring_axis)
    width = stored.shape[-1]
    chunks = stored.reshape(ring, -1, width)
    bits = ring.bit_length() - 1
    order = [sum(((place >> bit) & 1) << (bits - 1 - bit) for bit in range(bits)) for place in range(ring)]
    outgoing = chunks[jnp.array(order)].reshape(-1, width)
    incoming = lax.all_to_all(outgoing, ring_axis, 0, 0, tiled=True).reshape(ring, -1, width)
    own_holder = jnp.where(row == 0, owners[0], owners[1])
    other_holder = jnp.where(row == 0, owners[1], owners[0])
    mine = lax.dynamic_index_in_dim(incoming, own_holder % ring, 0, keepdims=False)
    theirs = lax.dynamic_index_in_dim(incoming, other_holder % ring, 0, keepdims=False)
    swap = [(0, 1), (1, 0)]
    got = lax.ppermute(theirs, row_axis, swap)
    flat = jnp.where(own_holder // ring == row, mine, got)
    apart = ring // 2
    while apart >= 1:
        side = (spot // apart) % 2
        route = [(low, low ^ apart) for low in range(ring)]
        other = lax.ppermute(flat, ring_axis, route)
        flat = jnp.where(
            side == 0,
            jnp.concatenate([flat, other], axis=0),
            jnp.concatenate([other, flat], axis=0),
        )
        apart //= 2
    other = lax.ppermute(flat, row_axis, swap)
    return flat.reshape(stored.shape), other.reshape(stored.shape), row


def butterfly_max(block, axis):
    count = lax.axis_size(axis)
    apart = count // 2
    while apart >= 1:
        route = [(low, low ^ apart) for low in range(count)]
        block = jnp.maximum(block, lax.ppermute(block, axis, route))
        apart //= 2
    return block


def from_partner(block, axis, apart):
    count = lax.axis_size(axis)
    route = []
    for low in range(count):
        high = low | 1 << apart
        if high != low and high < count:
            route += [(low, high), (high, low)]
    return lax.ppermute(block, axis, route)


def dft_table(length):
    positions = jnp.arange(length, dtype=jnp.int32)
    angles = (positions[:, None] * positions[None, :] % length).astype(jnp.float32) * (
        2.0 * math.pi / length
    )
    return jnp.concatenate([jnp.cos(angles), jnp.sin(angles)], axis=0).astype(jnp.bfloat16)


def twiddle(row_count, col_count):
    row_index = jnp.arange(row_count, dtype=jnp.int32)[:, None]
    col_index = jnp.arange(col_count, dtype=jnp.int32)[None, :]
    angles = (row_index * col_index % (row_count * col_count)).astype(jnp.float32) * (
        2.0 * math.pi / (row_count * col_count)
    )
    return (jnp.cos(angles), jnp.sin(angles))


def gate_mask(starts, widths, row_count, col_count):
    moment = (
        jnp.arange(row_count, dtype=jnp.int32)[:, None] * col_count
        + jnp.arange(col_count, dtype=jnp.int32)[None, :]
    )
    flags = jnp.zeros((row_count, col_count), dtype=jnp.bool_)
    for number in range(starts.shape[0]):
        flags = flags | (moment >= starts[number]) & (moment < starts[number] + widths[number])
    return flags


def filter_power(template, series, flags, first_table, second_table, twiddle_cos, twiddle_sin):
    count_a = template.shape[1]
    count_b = template.shape[2]
    out_rows = second_table.shape[0] // 2
    tmpl_re = template[0].astype(jnp.float32)
    tmpl_im = template[1].astype(jnp.float32)
    data_re = series[0].astype(jnp.float32)
    data_im = series[1].astype(jnp.float32)
    prod_re = data_re * tmpl_re + data_im * tmpl_im
    prod_im = data_im * tmpl_re - data_re * tmpl_im
    joined = jnp.concatenate([prod_re, prod_im], axis=1).astype(jnp.bfloat16)
    section_one = jnp.dot(first_table, joined, preferred_element_type=jnp.float32)
    section_re = section_one[:count_a, :count_b] - section_one[count_a:, count_b:]
    section_im = section_one[:count_a, count_b:] + section_one[count_a:, :count_b]
    turned = jnp.concatenate(
        [
            section_re * twiddle_cos - section_im * twiddle_sin,
            section_re * twiddle_sin + section_im * twiddle_cos,
        ],
        axis=0,
    ).astype(jnp.bfloat16)
    section_two = lax.dot_general(
        second_table, turned, (((1,), (1,)), ((), ())), preferred_element_type=jnp.float32
    )
    snr_re = section_two[:out_rows, :count_a] - section_two[out_rows:, count_a:]
    snr_im = section_two[:out_rows, count_a:] + section_two[out_rows:, :count_a]
    norm_sq = jnp.sum(tmpl_re * tmpl_re + tmpl_im * tmpl_im) + 1e-06
    snr_power = (snr_re * snr_re + snr_im * snr_im) / norm_sq
    return jnp.where(flags, 0.0, snr_power).astype(jnp.bfloat16)


def per_device(strain, bank, owners, gate_start, gate_width):
    count_a = strain.shape[2]
    count_b = strain.shape[3]
    block_count = owners.shape[1]
    half_rows = count_b // 2
    first_table = dft_table(count_a)
    second_table = dft_table(count_b)
    twiddle_cos, twiddle_sin = twiddle(count_a, count_b)
    flags = gate_mask(gate_start[0], gate_width[0], count_b, count_a)
    first_table, second_table, twiddle_cos, twiddle_sin, flags = lax.optimization_barrier(
        (first_table, second_table, twiddle_cos, twiddle_sin, flags)
    )
    series = strain[0]
    stored = bank[0]
    detector_side = lax.axis_index("z") % 2
    row_start = detector_side * half_rows
    own_tmpl, other_tmpl, side = spread(stored, owners[0], "xlo", "z")
    networks = []
    power = None
    for template in (own_tmpl, other_tmpl):
        if power is not None:
            template, power = lax.optimization_barrier((template, power))
        power = filter_power(
            template, series, flags, first_table, second_table, twiddle_cos, twiddle_sin
        )
        own_half = lax.dynamic_slice_in_dim(power, row_start, half_rows, 0)
        other_half = lax.dynamic_slice_in_dim(power, half_rows - row_start, half_rows, 0)
        partner = from_partner(other_half, "z", 0)
        networks.append(
            jnp.sqrt(own_half.astype(jnp.float32) + partner.astype(jnp.float32)).astype(
                jnp.bfloat16
            )
        )
    loudest = butterfly_max(jnp.maximum(networks[0], networks[1]), "tmpl")
    network = jnp.where(
        side == 0, jnp.stack([networks[0], networks[1]]), jnp.stack([networks[1], networks[0]])
    )
    network = network.reshape(block_count, 1, half_rows * count_a)
    loudest = loudest.reshape(1, half_rows * count_a)
    return (network, loudest)


def solution(mesh):
    tmpl_count = mesh.shape["tmpl"]
    seg_count = mesh.shape["seg"]
    grid = Mesh(mesh.devices.reshape(tmpl_count, 2, seg_count // 2), ("tmpl", "xlo", "z"))
    seg = ("xlo", "z")
    in_specs = (
        P(seg, None, None, None),
        P(("tmpl",) + seg, None, None, None),
        P("tmpl", None),
        P(seg, None),
        P(seg, None),
    )
    out_specs = (P("tmpl", seg, None), P(seg, None))
    return jax.shard_map(
        per_device, mesh=grid, in_specs=in_specs, out_specs=out_specs, check_vma=False
    )
```

```python
import math

import jax
import jax.numpy as jnp
from jax import lax
from jax.sharding import Mesh
from jax.sharding import PartitionSpec as P


def spread(stored, owners, row_axis, ring_axis):
    ring = lax.axis_size(ring_axis)
    row = lax.axis_index(row_axis)
    spot = lax.axis_index(ring_axis)
    width = stored.shape[-1]
    chunks = stored.reshape(ring, -1, width)
    bits = ring.bit_length() - 1
    order = [sum(((place >> bit) & 1) << (bits - 1 - bit) for bit in range(bits)) for place in range(ring)]
    outgoing = chunks[jnp.array(order)].reshape(-1, width)
    incoming = lax.all_to_all(outgoing, ring_axis, 0, 0, tiled=True).reshape(ring, -1, width)
    picked = jnp.stack(
        [lax.dynamic_index_in_dim(incoming, holder % ring, 0, keepdims=False) for holder in owners]
    )
    got = lax.ppermute(picked, row_axis, [(0, 1), (1, 0)])
    here = jnp.stack([holder // ring == row for holder in owners])
    flat = jnp.where(here[:, None, None], picked, got)
    apart = ring // 2
    while apart >= 1:
        side = (spot // apart) % 2
        route = [(low, low ^ apart) for low in range(ring)]
        other = lax.ppermute(flat, ring_axis, route)
        flat = jnp.where(
            side == 0,
            jnp.concatenate([flat, other], axis=1),
            jnp.concatenate([other, flat], axis=1),
        )
        apart //= 2
    return flat.reshape((len(owners),) + stored.shape)


def butterfly_max(block, axis):
    count = lax.axis_size(axis)
    apart = count // 2
    while apart >= 1:
        route = [(low, low ^ apart) for low in range(count)]
        block = jnp.maximum(block, lax.ppermute(block, axis, route))
        apart //= 2
    return block


def from_partner(block, axis, apart):
    count = lax.axis_size(axis)
    route = []
    for low in range(count):
        high = low | 1 << apart
        if high != low and high < count:
            route += [(low, high), (high, low)]
    return lax.ppermute(block, axis, route)


def dft_table(length):
    positions = jnp.arange(length, dtype=jnp.int32)
    angles = (positions[:, None] * positions[None, :] % length).astype(jnp.float32) * (
        2.0 * math.pi / length
    )
    return jnp.concatenate([jnp.cos(angles), jnp.sin(angles)], axis=0).astype(jnp.bfloat16)


def twiddle(row_count, col_count):
    row_index = jnp.arange(row_count, dtype=jnp.int32)[:, None]
    col_index = jnp.arange(col_count, dtype=jnp.int32)[None, :]
    angles = (row_index * col_index % (row_count * col_count)).astype(jnp.float32) * (
        2.0 * math.pi / (row_count * col_count)
    )
    return (jnp.cos(angles), jnp.sin(angles))


def gate_mask(starts, widths, row_count, col_count):
    moment = (
        jnp.arange(row_count, dtype=jnp.int32)[:, None] * col_count
        + jnp.arange(col_count, dtype=jnp.int32)[None, :]
    )
    flags = jnp.zeros((row_count, col_count), dtype=jnp.bool_)
    for number in range(starts.shape[0]):
        flags = flags | (moment >= starts[number]) & (moment < starts[number] + widths[number])
    return flags


def filter_power(template, series, flags, first_table, second_table, twiddle_cos, twiddle_sin):
    count_a = template.shape[1]
    count_b = template.shape[2]
    out_rows = second_table.shape[0] // 2
    tmpl_re = template[0].astype(jnp.float32)
    tmpl_im = template[1].astype(jnp.float32)
    data_re = series[0].astype(jnp.float32)
    data_im = series[1].astype(jnp.float32)
    prod_re = data_re * tmpl_re + data_im * tmpl_im
    prod_im = data_im * tmpl_re - data_re * tmpl_im
    joined = jnp.concatenate([prod_re, prod_im], axis=1).astype(jnp.bfloat16)
    section_one = jnp.dot(first_table, joined, preferred_element_type=jnp.float32)
    section_re = section_one[:count_a, :count_b] - section_one[count_a:, count_b:]
    section_im = section_one[:count_a, count_b:] + section_one[count_a:, :count_b]
    turned = jnp.concatenate(
        [
            section_re * twiddle_cos - section_im * twiddle_sin,
            section_re * twiddle_sin + section_im * twiddle_cos,
        ],
        axis=0,
    ).astype(jnp.bfloat16)
    section_two = lax.dot_general(
        second_table, turned, (((1,), (1,)), ((), ())), preferred_element_type=jnp.float32
    )
    snr_re = section_two[:out_rows, :count_a] - section_two[out_rows:, count_a:]
    snr_im = section_two[:out_rows, count_a:] + section_two[out_rows:, :count_a]
    norm_sq = jnp.sum(tmpl_re * tmpl_re + tmpl_im * tmpl_im) + 1e-06
    snr_power = (snr_re * snr_re + snr_im * snr_im) / norm_sq
    return jnp.where(flags, 0.0, snr_power).astype(jnp.bfloat16)


def per_device(strain, bank, owners, gate_start, gate_width):
    count_a = strain.shape[2]
    count_b = strain.shape[3]
    block_count = owners.shape[1]
    half_rows = count_b // 2
    first_table = dft_table(count_a)
    second_table = dft_table(count_b)
    twiddle_cos, twiddle_sin = twiddle(count_a, count_b)
    flags = gate_mask(gate_start[0], gate_width[0], count_b, count_a)
    first_table, second_table, twiddle_cos, twiddle_sin, flags = lax.optimization_barrier(
        (first_table, second_table, twiddle_cos, twiddle_sin, flags)
    )
    series = strain[0]
    stored = bank[0]
    detector_side = lax.axis_index("z") % 2
    row_start = detector_side * half_rows
    templates = spread(stored, [owners[0, n] for n in range(block_count)], "xlo", "z")
    networks = []
    power = None
    for number in range(block_count):
        template = templates[number]
        if power is not None:
            template, power = lax.optimization_barrier((template, power))
        power = filter_power(
            template, series, flags, first_table, second_table, twiddle_cos, twiddle_sin
        )
        own_half = lax.dynamic_slice_in_dim(power, row_start, half_rows, 0)
        other_half = lax.dynamic_slice_in_dim(power, half_rows - row_start, half_rows, 0)
        partner = from_partner(other_half, "z", 0)
        networks.append(
            jnp.sqrt(own_half.astype(jnp.float32) + partner.astype(jnp.float32)).astype(
                jnp.bfloat16
            )
        )
    network = jnp.stack(networks)
    loudest = butterfly_max(jnp.max(network, axis=0), "tmpl")
    network = network.reshape(block_count, 1, half_rows * count_a)
    loudest = loudest.reshape(1, half_rows * count_a)
    return (network, loudest)


def solution(mesh):
    tmpl_count = mesh.shape["tmpl"]
    seg_count = mesh.shape["seg"]
    grid = Mesh(mesh.devices.reshape(tmpl_count, 2, seg_count // 2), ("tmpl", "xlo", "z"))
    seg = ("xlo", "z")
    in_specs = (
        P(seg, None, None, None),
        P(("tmpl",) + seg, None, None, None),
        P("tmpl", None),
        P(seg, None),
        P(seg, None),
    )
    out_specs = (P("tmpl", seg, None), P(seg, None))
    return jax.shard_map(
        per_device, mesh=grid, in_specs=in_specs, out_specs=out_specs, check_vma=False
    )
```

```python
import math

import jax
import jax.numpy as jnp
from jax import lax
from jax.experimental import pallas as pl
from jax.experimental.pallas import tpu as pltpu
from jax.sharding import Mesh
from jax.sharding import PartitionSpec as P


def spread(stored, owners, row_axis, ring_axis):
    ring = lax.axis_size(ring_axis)
    row = lax.axis_index(row_axis)
    spot = lax.axis_index(ring_axis)
    width = stored.shape[-1]
    chunks = stored.reshape(ring, -1, width)
    bits = ring.bit_length() - 1
    order = [sum(((place >> bit) & 1) << (bits - 1 - bit) for bit in range(bits)) for place in range(ring)]
    outgoing = chunks[jnp.array(order)].reshape(-1, width)
    incoming = lax.all_to_all(outgoing, ring_axis, 0, 0, tiled=True).reshape(ring, -1, width)
    own_holder = jnp.where(row == 0, owners[0], owners[1])
    other_holder = jnp.where(row == 0, owners[1], owners[0])
    mine = lax.dynamic_index_in_dim(incoming, own_holder % ring, 0, keepdims=False)
    theirs = lax.dynamic_index_in_dim(incoming, other_holder % ring, 0, keepdims=False)
    swap = [(0, 1), (1, 0)]
    got = lax.ppermute(theirs, row_axis, swap)
    flat = jnp.where(own_holder // ring == row, mine, got)
    apart = ring // 2
    while apart >= 1:
        side = (spot // apart) % 2
        route = [(low, low ^ apart) for low in range(ring)]
        other = lax.ppermute(flat, ring_axis, route)
        flat = jnp.where(
            side == 0,
            jnp.concatenate([flat, other], axis=0),
            jnp.concatenate([other, flat], axis=0),
        )
        apart //= 2
    other = lax.ppermute(flat, row_axis, swap)
    return flat.reshape(stored.shape), other.reshape(stored.shape), row


def butterfly_max(block, axis):
    count = lax.axis_size(axis)
    apart = count // 2
    while apart >= 1:
        route = [(low, low ^ apart) for low in range(count)]
        block = jnp.maximum(block, lax.ppermute(block, axis, route))
        apart //= 2
    return block


def from_partner(block, axis, apart):
    count = lax.axis_size(axis)
    route = []
    for low in range(count):
        high = low | 1 << apart
        if high != low and high < count:
            route += [(low, high), (high, low)]
    return lax.ppermute(block, axis, route)


def dft_table(length):
    positions = jnp.arange(length, dtype=jnp.int32)
    angles = (positions[:, None] * positions[None, :] % length).astype(jnp.float32) * (
        2.0 * math.pi / length
    )
    return jnp.concatenate([jnp.cos(angles), jnp.sin(angles)], axis=0).astype(jnp.bfloat16)


def twiddle(row_count, col_count):
    row_index = jnp.arange(row_count, dtype=jnp.int32)[:, None]
    col_index = jnp.arange(col_count, dtype=jnp.int32)[None, :]
    angles = (row_index * col_index % (row_count * col_count)).astype(jnp.float32) * (
        2.0 * math.pi / (row_count * col_count)
    )
    return (jnp.cos(angles), jnp.sin(angles))


def gate_mask(starts, widths, row_count, col_count):
    moment = (
        jnp.arange(row_count, dtype=jnp.int32)[:, None] * col_count
        + jnp.arange(col_count, dtype=jnp.int32)[None, :]
    )
    flags = jnp.zeros((row_count, col_count), dtype=jnp.bool_)
    for number in range(starts.shape[0]):
        flags = flags | (moment >= starts[number]) & (moment < starts[number] + widths[number])
    return flags


def filter_power(template, series, flags, first_table, second_table, twiddle_cos, twiddle_sin):
    count_a = template.shape[1]
    count_b = template.shape[2]
    out_rows = second_table.shape[0] // 2
    tmpl_re = template[0].astype(jnp.float32)
    tmpl_im = template[1].astype(jnp.float32)
    data_re = series[0].astype(jnp.float32)
    data_im = series[1].astype(jnp.float32)
    prod_re = data_re * tmpl_re + data_im * tmpl_im
    prod_im = data_im * tmpl_re - data_re * tmpl_im
    joined = jnp.concatenate([prod_re, prod_im], axis=1).astype(jnp.bfloat16)
    section_one = jnp.dot(first_table, joined, preferred_element_type=jnp.float32)
    section_re = section_one[:count_a, :count_b] - section_one[count_a:, count_b:]
    section_im = section_one[:count_a, count_b:] + section_one[count_a:, :count_b]
    turned = jnp.concatenate(
        [
            section_re * twiddle_cos - section_im * twiddle_sin,
            section_re * twiddle_sin + section_im * twiddle_cos,
        ],
        axis=0,
    ).astype(jnp.bfloat16)
    section_two = lax.dot_general(
        second_table, turned, (((1,), (1,)), ((), ())), preferred_element_type=jnp.float32
    )
    snr_re = section_two[:out_rows, :count_a] - section_two[out_rows:, count_a:]
    snr_im = section_two[:out_rows, count_a:] + section_two[out_rows:, :count_a]
    norm_sq = jnp.sum(tmpl_re * tmpl_re + tmpl_im * tmpl_im) + 1e-06
    snr_power = (snr_re * snr_re + snr_im * snr_im) / norm_sq
    return jnp.where(flags, 0.0, snr_power).astype(jnp.bfloat16)


def filter_kernel(
    template_ref, series_ref, first_ref, second_ref, cos_ref, sin_ref, start_ref, width_ref, out_ref
):
    count_a = template_ref.shape[1]
    count_b = template_ref.shape[2]
    out_rows = second_ref.shape[0] // 2
    tmpl_re = template_ref[0].astype(jnp.float32)
    tmpl_im = template_ref[1].astype(jnp.float32)
    data_re = series_ref[0].astype(jnp.float32)
    data_im = series_ref[1].astype(jnp.float32)
    prod_re = (data_re * tmpl_re + data_im * tmpl_im).astype(jnp.bfloat16)
    prod_im = (data_im * tmpl_re - data_re * tmpl_im).astype(jnp.bfloat16)
    first = first_ref[...]
    left = jnp.dot(first, prod_re, preferred_element_type=jnp.float32)
    right = jnp.dot(first, prod_im, preferred_element_type=jnp.float32)
    section_re = left[:count_a] - right[count_a:]
    section_im = right[:count_a] + left[count_a:]
    turn_cos = cos_ref[...]
    turn_sin = sin_ref[...]
    turned_re = (section_re * turn_cos - section_im * turn_sin).astype(jnp.bfloat16)
    turned_im = (section_re * turn_sin + section_im * turn_cos).astype(jnp.bfloat16)
    second = second_ref[...]
    contract = (((1,), (1,)), ((), ()))
    left = lax.dot_general(second, turned_re, contract, preferred_element_type=jnp.float32)
    right = lax.dot_general(second, turned_im, contract, preferred_element_type=jnp.float32)
    snr_re = left[:out_rows] - right[out_rows:]
    snr_im = right[:out_rows] + left[out_rows:]
    norm_sq = jnp.sum(tmpl_re * tmpl_re + tmpl_im * tmpl_im) + 1e-06
    snr_power = (snr_re * snr_re + snr_im * snr_im) / norm_sq
    moment = (
        lax.broadcasted_iota(jnp.int32, snr_power.shape, 0) * count_a
        + lax.broadcasted_iota(jnp.int32, snr_power.shape, 1)
    )
    flags = jnp.zeros(snr_power.shape, dtype=jnp.bool_)
    for number in range(start_ref.shape[0]):
        begin = start_ref[number]
        flags = flags | (moment >= begin) & (moment < begin + width_ref[number])
    out_ref[...] = jnp.where(flags, 0.0, snr_power).astype(jnp.bfloat16)


def filter_call(template, series, first_table, second_table, twiddle_cos, twiddle_sin, starts, widths):
    vmem = pltpu.MemorySpace.VMEM
    smem = pltpu.MemorySpace.SMEM
    rows = second_table.shape[0] // 2
    return pl.pallas_call(
        filter_kernel,
        out_shape=jax.ShapeDtypeStruct((rows, template.shape[1]), jnp.bfloat16),
        in_specs=[pl.BlockSpec(memory_space=vmem)] * 6 + [pl.BlockSpec(memory_space=smem)] * 2,
        out_specs=pl.BlockSpec(memory_space=vmem),
        compiler_params=pltpu.CompilerParams(vmem_limit_bytes=48 * 1024 * 1024),
    )(template, series, first_table, second_table, twiddle_cos, twiddle_sin, starts, widths)


def per_device(strain, bank, owners, gate_start, gate_width):
    count_a = strain.shape[2]
    count_b = strain.shape[3]
    block_count = owners.shape[1]
    half_rows = count_b // 2
    first_table = dft_table(count_a)
    second_table = dft_table(count_b)
    twiddle_cos, twiddle_sin = twiddle(count_a, count_b)
    first_table, second_table, twiddle_cos, twiddle_sin = lax.optimization_barrier(
        (first_table, second_table, twiddle_cos, twiddle_sin)
    )
    series = strain[0]
    stored = bank[0]
    detector_side = lax.axis_index("z") % 2
    row_start = detector_side * half_rows
    own_tmpl, other_tmpl, side = spread(stored, owners[0], "xlo", "z")
    networks = []
    power = None
    for template in (own_tmpl, other_tmpl):
        if power is not None:
            template, power = lax.optimization_barrier((template, power))
        power = filter_call(
            template,
            series,
            first_table,
            second_table,
            twiddle_cos,
            twiddle_sin,
            gate_start[0],
            gate_width[0],
        )
        own_half = lax.dynamic_slice_in_dim(power, row_start, half_rows, 0)
        other_half = lax.dynamic_slice_in_dim(power, half_rows - row_start, half_rows, 0)
        partner = from_partner(other_half, "z", 0)
        networks.append(
            jnp.sqrt(own_half.astype(jnp.float32) + partner.astype(jnp.float32)).astype(
                jnp.bfloat16
            )
        )
    loudest = butterfly_max(jnp.maximum(networks[0], networks[1]), "tmpl")
    network = jnp.where(
        side == 0, jnp.stack([networks[0], networks[1]]), jnp.stack([networks[1], networks[0]])
    )
    network = network.reshape(block_count, 1, half_rows * count_a)
    loudest = loudest.reshape(1, half_rows * count_a)
    return (network, loudest)


def solution(mesh):
    tmpl_count = mesh.shape["tmpl"]
    seg_count = mesh.shape["seg"]
    grid = Mesh(mesh.devices.reshape(tmpl_count, 2, seg_count // 2), ("tmpl", "xlo", "z"))
    seg = ("xlo", "z")
    in_specs = (
        P(seg, None, None, None),
        P(("tmpl",) + seg, None, None, None),
        P("tmpl", None),
        P(seg, None),
        P(seg, None),
    )
    out_specs = (P("tmpl", seg, None), P(seg, None))
    return jax.shard_map(
        per_device, mesh=grid, in_specs=in_specs, out_specs=out_specs, check_vma=False
    )
```

```python
import math

import jax
import jax.numpy as jnp
from jax import lax
from jax.experimental import pallas as pl
from jax.experimental.pallas import tpu as pltpu
from jax.sharding import Mesh
from jax.sharding import PartitionSpec as P


def spread(stored, owners, row_axis, ring_axis, riders):
    ring = lax.axis_size(ring_axis)
    row = lax.axis_index(row_axis)
    spot = lax.axis_index(ring_axis)
    width = stored.shape[-1]
    chunks = stored.reshape(ring, -1, width)
    bits = ring.bit_length() - 1
    order = [sum(((place >> bit) & 1) << (bits - 1 - bit) for bit in range(bits)) for place in range(ring)]
    outgoing = chunks[jnp.array(order)].reshape(-1, width)
    incoming = lax.all_to_all(outgoing, ring_axis, 0, 0, tiled=True).reshape(ring, -1, width)
    own_holder = jnp.where(row == 0, owners[0], owners[1])
    other_holder = jnp.where(row == 0, owners[1], owners[0])
    mine = lax.dynamic_index_in_dim(incoming, own_holder % ring, 0, keepdims=False)
    theirs = lax.dynamic_index_in_dim(incoming, other_holder % ring, 0, keepdims=False)
    swap = [(0, 1), (1, 0)]
    got = lax.ppermute(theirs, row_axis, swap)
    flat = jnp.where(own_holder // ring == row, mine, got)
    flat, riders = lax.optimization_barrier((flat, riders))
    apart = ring // 2
    while apart >= 1:
        side = (spot // apart) % 2
        route = [(low, low ^ apart) for low in range(ring)]
        other = lax.ppermute(flat, ring_axis, route)
        flat = jnp.where(
            side == 0,
            jnp.concatenate([flat, other], axis=0),
            jnp.concatenate([other, flat], axis=0),
        )
        apart //= 2
    other = lax.ppermute(flat, row_axis, swap)
    return flat.reshape(stored.shape), other.reshape(stored.shape), row, riders


def butterfly_max(block, axis):
    count = lax.axis_size(axis)
    apart = count // 2
    while apart >= 1:
        route = [(low, low ^ apart) for low in range(count)]
        block = jnp.maximum(block, lax.ppermute(block, axis, route))
        apart //= 2
    return block


def from_partner(block, axis, apart):
    count = lax.axis_size(axis)
    route = []
    for low in range(count):
        high = low | 1 << apart
        if high != low and high < count:
            route += [(low, high), (high, low)]
    return lax.ppermute(block, axis, route)


def dft_table(length):
    positions = jnp.arange(length, dtype=jnp.int32)
    angles = (positions[:, None] * positions[None, :] % length).astype(jnp.float32) * (
        2.0 * math.pi / length
    )
    return jnp.concatenate([jnp.cos(angles), jnp.sin(angles)], axis=0).astype(jnp.bfloat16)


def twiddle(row_count, col_count):
    row_index = jnp.arange(row_count, dtype=jnp.int32)[:, None]
    col_index = jnp.arange(col_count, dtype=jnp.int32)[None, :]
    angles = (row_index * col_index % (row_count * col_count)).astype(jnp.float32) * (
        2.0 * math.pi / (row_count * col_count)
    )
    return (jnp.cos(angles), jnp.sin(angles))


def gate_mask(starts, widths, row_count, col_count):
    moment = (
        jnp.arange(row_count, dtype=jnp.int32)[:, None] * col_count
        + jnp.arange(col_count, dtype=jnp.int32)[None, :]
    )
    flags = jnp.zeros((row_count, col_count), dtype=jnp.bool_)
    for number in range(starts.shape[0]):
        flags = flags | (moment >= starts[number]) & (moment < starts[number] + widths[number])
    return flags


def filter_power(template, series, flags, first_table, second_table, twiddle_cos, twiddle_sin):
    count_a = template.shape[1]
    count_b = template.shape[2]
    out_rows = second_table.shape[0] // 2
    tmpl_re = template[0].astype(jnp.float32)
    tmpl_im = template[1].astype(jnp.float32)
    data_re = series[0].astype(jnp.float32)
    data_im = series[1].astype(jnp.float32)
    prod_re = data_re * tmpl_re + data_im * tmpl_im
    prod_im = data_im * tmpl_re - data_re * tmpl_im
    joined = jnp.concatenate([prod_re, prod_im], axis=1).astype(jnp.bfloat16)
    section_one = jnp.dot(first_table, joined, preferred_element_type=jnp.float32)
    section_re = section_one[:count_a, :count_b] - section_one[count_a:, count_b:]
    section_im = section_one[:count_a, count_b:] + section_one[count_a:, :count_b]
    turned = jnp.concatenate(
        [
            section_re * twiddle_cos - section_im * twiddle_sin,
            section_re * twiddle_sin + section_im * twiddle_cos,
        ],
        axis=0,
    ).astype(jnp.bfloat16)
    section_two = lax.dot_general(
        second_table, turned, (((1,), (1,)), ((), ())), preferred_element_type=jnp.float32
    )
    snr_re = section_two[:out_rows, :count_a] - section_two[out_rows:, count_a:]
    snr_im = section_two[:out_rows, count_a:] + section_two[out_rows:, :count_a]
    norm_sq = jnp.sum(tmpl_re * tmpl_re + tmpl_im * tmpl_im) + 1e-06
    snr_power = (snr_re * snr_re + snr_im * snr_im) / norm_sq
    return jnp.where(flags, 0.0, snr_power).astype(jnp.bfloat16)


def filter_kernel(
    template_ref, series_ref, first_ref, second_ref, cos_ref, sin_ref, start_ref, width_ref, out_ref
):
    count_a = template_ref.shape[1]
    count_b = template_ref.shape[2]
    out_rows = second_ref.shape[0] // 2
    tmpl_re = template_ref[0].astype(jnp.float32)
    tmpl_im = template_ref[1].astype(jnp.float32)
    data_re = series_ref[0].astype(jnp.float32)
    data_im = series_ref[1].astype(jnp.float32)
    prod_re = (data_re * tmpl_re + data_im * tmpl_im).astype(jnp.bfloat16)
    prod_im = (data_im * tmpl_re - data_re * tmpl_im).astype(jnp.bfloat16)
    first = first_ref[...]
    left = jnp.dot(first, prod_re, preferred_element_type=jnp.float32)
    right = jnp.dot(first, prod_im, preferred_element_type=jnp.float32)
    section_re = left[:count_a] - right[count_a:]
    section_im = right[:count_a] + left[count_a:]
    turn_cos = cos_ref[...]
    turn_sin = sin_ref[...]
    turned_re = (section_re * turn_cos - section_im * turn_sin).astype(jnp.bfloat16)
    turned_im = (section_re * turn_sin + section_im * turn_cos).astype(jnp.bfloat16)
    second = second_ref[...]
    contract = (((1,), (1,)), ((), ()))
    left = lax.dot_general(second, turned_re, contract, preferred_element_type=jnp.float32)
    right = lax.dot_general(second, turned_im, contract, preferred_element_type=jnp.float32)
    snr_re = left[:out_rows] - right[out_rows:]
    snr_im = right[:out_rows] + left[out_rows:]
    norm_sq = jnp.sum(tmpl_re * tmpl_re + tmpl_im * tmpl_im) + 1e-06
    snr_power = (snr_re * snr_re + snr_im * snr_im) / norm_sq
    moment = (
        lax.broadcasted_iota(jnp.int32, snr_power.shape, 0) * count_a
        + lax.broadcasted_iota(jnp.int32, snr_power.shape, 1)
    )
    flags = jnp.zeros(snr_power.shape, dtype=jnp.bool_)
    for number in range(start_ref.shape[0]):
        begin = start_ref[number]
        flags = flags | (moment >= begin) & (moment < begin + width_ref[number])
    out_ref[...] = jnp.where(flags, 0.0, snr_power).astype(jnp.bfloat16)


def filter_call(template, series, first_table, second_table, twiddle_cos, twiddle_sin, starts, widths):
    vmem = pltpu.MemorySpace.VMEM
    smem = pltpu.MemorySpace.SMEM
    rows = second_table.shape[0] // 2
    return pl.pallas_call(
        filter_kernel,
        out_shape=jax.ShapeDtypeStruct((rows, template.shape[1]), jnp.bfloat16),
        in_specs=[pl.BlockSpec(memory_space=vmem)] * 6 + [pl.BlockSpec(memory_space=smem)] * 2,
        out_specs=pl.BlockSpec(memory_space=vmem),
        compiler_params=pltpu.CompilerParams(vmem_limit_bytes=48 * 1024 * 1024),
    )(template, series, first_table, second_table, twiddle_cos, twiddle_sin, starts, widths)


def per_device(strain, bank, owners, gate_start, gate_width):
    count_a = strain.shape[2]
    count_b = strain.shape[3]
    block_count = owners.shape[1]
    half_rows = count_b // 2
    first_table = dft_table(count_a)
    second_table = dft_table(count_b)
    twiddle_cos, twiddle_sin = twiddle(count_a, count_b)
    series = strain[0]
    stored = bank[0]
    detector_side = lax.axis_index("z") % 2
    row_start = detector_side * half_rows
    own_tmpl, other_tmpl, side, tables = spread(
        stored, owners[0], "xlo", "z", (first_table, second_table, twiddle_cos, twiddle_sin)
    )
    first_table, second_table, twiddle_cos, twiddle_sin = tables
    networks = []
    power = None
    for template in (own_tmpl, other_tmpl):
        if power is not None:
            template, power = lax.optimization_barrier((template, power))
        power = filter_call(
            template,
            series,
            first_table,
            second_table,
            twiddle_cos,
            twiddle_sin,
            gate_start[0],
            gate_width[0],
        )
        own_half = lax.dynamic_slice_in_dim(power, row_start, half_rows, 0)
        other_half = lax.dynamic_slice_in_dim(power, half_rows - row_start, half_rows, 0)
        partner = from_partner(other_half, "z", 0)
        networks.append(
            jnp.sqrt(own_half.astype(jnp.float32) + partner.astype(jnp.float32)).astype(
                jnp.bfloat16
            )
        )
    loudest = butterfly_max(jnp.maximum(networks[0], networks[1]), "tmpl")
    network = jnp.where(
        side == 0, jnp.stack([networks[0], networks[1]]), jnp.stack([networks[1], networks[0]])
    )
    network = network.reshape(block_count, 1, half_rows * count_a)
    loudest = loudest.reshape(1, half_rows * count_a)
    return (network, loudest)


def solution(mesh):
    tmpl_count = mesh.shape["tmpl"]
    seg_count = mesh.shape["seg"]
    grid = Mesh(mesh.devices.reshape(tmpl_count, 2, seg_count // 2), ("tmpl", "xlo", "z"))
    seg = ("xlo", "z")
    in_specs = (
        P(seg, None, None, None),
        P(("tmpl",) + seg, None, None, None),
        P("tmpl", None),
        P(seg, None),
        P(seg, None),
    )
    out_specs = (P("tmpl", seg, None), P(seg, None))
    return jax.shard_map(
        per_device, mesh=grid, in_specs=in_specs, out_specs=out_specs, check_vma=False
    )
```

```python
import math

import jax
import jax.numpy as jnp
from jax import lax
from jax.experimental import pallas as pl
from jax.experimental.pallas import tpu as pltpu
from jax.sharding import Mesh
from jax.sharding import PartitionSpec as P


def spread(stored, owners, row_axis, ring_axis, riders, early):
    ring = lax.axis_size(ring_axis)
    row = lax.axis_index(row_axis)
    spot = lax.axis_index(ring_axis)
    width = stored.shape[-1]
    chunks = stored.reshape(ring, -1, width)
    bits = ring.bit_length() - 1
    order = [sum(((place >> bit) & 1) << (bits - 1 - bit) for bit in range(bits)) for place in range(ring)]
    outgoing = chunks[jnp.array(order)].reshape(-1, width)
    incoming = lax.all_to_all(outgoing, ring_axis, 0, 0, tiled=True).reshape(ring, -1, width)
    incoming, early = lax.optimization_barrier((incoming, early))
    own_holder = jnp.where(row == 0, owners[0], owners[1])
    other_holder = jnp.where(row == 0, owners[1], owners[0])
    mine = lax.dynamic_index_in_dim(incoming, own_holder % ring, 0, keepdims=False)
    theirs = lax.dynamic_index_in_dim(incoming, other_holder % ring, 0, keepdims=False)
    swap = [(0, 1), (1, 0)]
    got = lax.ppermute(theirs, row_axis, swap)
    flat = jnp.where(own_holder // ring == row, mine, got)
    flat, riders = lax.optimization_barrier((flat, riders))
    apart = ring // 2
    while apart >= 1:
        side = (spot // apart) % 2
        route = [(low, low ^ apart) for low in range(ring)]
        other = lax.ppermute(flat, ring_axis, route)
        flat = jnp.where(
            side == 0,
            jnp.concatenate([flat, other], axis=0),
            jnp.concatenate([other, flat], axis=0),
        )
        apart //= 2
    other = lax.ppermute(flat, row_axis, swap)
    return flat.reshape(stored.shape), other.reshape(stored.shape), row, riders, early


def butterfly_max(block, axis):
    count = lax.axis_size(axis)
    apart = count // 2
    while apart >= 1:
        route = [(low, low ^ apart) for low in range(count)]
        block = jnp.maximum(block, lax.ppermute(block, axis, route))
        apart //= 2
    return block


def from_partner(block, axis, apart):
    count = lax.axis_size(axis)
    route = []
    for low in range(count):
        high = low | 1 << apart
        if high != low and high < count:
            route += [(low, high), (high, low)]
    return lax.ppermute(block, axis, route)


def dft_table(length):
    positions = jnp.arange(length, dtype=jnp.int32)
    angles = (positions[:, None] * positions[None, :] % length).astype(jnp.float32) * (
        2.0 * math.pi / length
    )
    return jnp.concatenate([jnp.cos(angles), jnp.sin(angles)], axis=0).astype(jnp.bfloat16)


def twiddle(row_count, col_count):
    row_index = jnp.arange(row_count, dtype=jnp.int32)[:, None]
    col_index = jnp.arange(col_count, dtype=jnp.int32)[None, :]
    angles = (row_index * col_index % (row_count * col_count)).astype(jnp.float32) * (
        2.0 * math.pi / (row_count * col_count)
    )
    return (jnp.cos(angles), jnp.sin(angles))


def gate_mask(starts, widths, row_count, col_count):
    moment = (
        jnp.arange(row_count, dtype=jnp.int32)[:, None] * col_count
        + jnp.arange(col_count, dtype=jnp.int32)[None, :]
    )
    flags = jnp.zeros((row_count, col_count), dtype=jnp.bool_)
    for number in range(starts.shape[0]):
        flags = flags | (moment >= starts[number]) & (moment < starts[number] + widths[number])
    return flags


def filter_power(template, series, flags, first_table, second_table, twiddle_cos, twiddle_sin):
    count_a = template.shape[1]
    count_b = template.shape[2]
    out_rows = second_table.shape[0] // 2
    tmpl_re = template[0].astype(jnp.float32)
    tmpl_im = template[1].astype(jnp.float32)
    data_re = series[0].astype(jnp.float32)
    data_im = series[1].astype(jnp.float32)
    prod_re = data_re * tmpl_re + data_im * tmpl_im
    prod_im = data_im * tmpl_re - data_re * tmpl_im
    joined = jnp.concatenate([prod_re, prod_im], axis=1).astype(jnp.bfloat16)
    section_one = jnp.dot(first_table, joined, preferred_element_type=jnp.float32)
    section_re = section_one[:count_a, :count_b] - section_one[count_a:, count_b:]
    section_im = section_one[:count_a, count_b:] + section_one[count_a:, :count_b]
    turned = jnp.concatenate(
        [
            section_re * twiddle_cos - section_im * twiddle_sin,
            section_re * twiddle_sin + section_im * twiddle_cos,
        ],
        axis=0,
    ).astype(jnp.bfloat16)
    section_two = lax.dot_general(
        second_table, turned, (((1,), (1,)), ((), ())), preferred_element_type=jnp.float32
    )
    snr_re = section_two[:out_rows, :count_a] - section_two[out_rows:, count_a:]
    snr_im = section_two[:out_rows, count_a:] + section_two[out_rows:, :count_a]
    norm_sq = jnp.sum(tmpl_re * tmpl_re + tmpl_im * tmpl_im) + 1e-06
    snr_power = (snr_re * snr_re + snr_im * snr_im) / norm_sq
    return jnp.where(flags, 0.0, snr_power).astype(jnp.bfloat16)


def series_power(template_re, template_im, series_ref, first, second, turn_cos, turn_sin, starts, widths, row0):
    count_a = template_re.shape[0]
    out_rows = second.shape[0] // 2
    data_re = series_ref[0].astype(jnp.float32)
    data_im = series_ref[1].astype(jnp.float32)
    prod_re = (data_re * template_re + data_im * template_im).astype(jnp.bfloat16)
    prod_im = (data_im * template_re - data_re * template_im).astype(jnp.bfloat16)
    left = jnp.dot(first, prod_re, preferred_element_type=jnp.float32)
    right = jnp.dot(first, prod_im, preferred_element_type=jnp.float32)
    section_re = left[:count_a] - right[count_a:]
    section_im = right[:count_a] + left[count_a:]
    turned_re = (section_re * turn_cos - section_im * turn_sin).astype(jnp.bfloat16)
    turned_im = (section_re * turn_sin + section_im * turn_cos).astype(jnp.bfloat16)
    contract = (((1,), (1,)), ((), ()))
    left = lax.dot_general(second, turned_re, contract, preferred_element_type=jnp.float32)
    right = lax.dot_general(second, turned_im, contract, preferred_element_type=jnp.float32)
    snr_re = left[:out_rows] - right[out_rows:]
    snr_im = right[:out_rows] + left[out_rows:]
    norm_sq = jnp.sum(template_re * template_re + template_im * template_im) + 1e-06
    snr_power = (snr_re * snr_re + snr_im * snr_im) / norm_sq
    moment = (
        lax.broadcasted_iota(jnp.int32, snr_power.shape, 0) + row0
    ) * count_a + lax.broadcasted_iota(jnp.int32, snr_power.shape, 1)
    flags = jnp.zeros(snr_power.shape, dtype=jnp.bool_)
    for number in range(starts.shape[0]):
        begin = starts[number]
        flags = flags | (moment >= begin) & (moment < begin + widths[number])
    return jnp.where(flags, 0.0, snr_power).astype(jnp.bfloat16)


def network_kernel(
    template_ref,
    mine_ref,
    partner_ref,
    first_ref,
    second_ref,
    cos_ref,
    sin_ref,
    mine_start_ref,
    mine_width_ref,
    partner_start_ref,
    partner_width_ref,
    row_ref,
    out_ref,
):
    template_re = template_ref[0].astype(jnp.float32)
    template_im = template_ref[1].astype(jnp.float32)
    first = first_ref[...]
    second = second_ref[...]
    turn_cos = cos_ref[...]
    turn_sin = sin_ref[...]
    row0 = row_ref[0]
    powers = [
        series_power(
            template_re, template_im, series, first, second, turn_cos, turn_sin, starts, widths, row0
        )
        for series, starts, widths in (
            (mine_ref, mine_start_ref, mine_width_ref),
            (partner_ref, partner_start_ref, partner_width_ref),
        )
    ]
    total = powers[0].astype(jnp.float32) + powers[1].astype(jnp.float32)
    out_ref[...] = jnp.sqrt(total).astype(jnp.bfloat16)


def network_call(template, mine, partner, first_table, second_half, twiddle_cos, twiddle_sin, gates, row0):
    vmem = pltpu.MemorySpace.VMEM
    smem = pltpu.MemorySpace.SMEM
    rows = second_half.shape[0] // 2
    return pl.pallas_call(
        network_kernel,
        out_shape=jax.ShapeDtypeStruct((rows, template.shape[1]), jnp.bfloat16),
        in_specs=[pl.BlockSpec(memory_space=vmem)] * 7 + [pl.BlockSpec(memory_space=smem)] * 5,
        out_specs=pl.BlockSpec(memory_space=vmem),
        compiler_params=pltpu.CompilerParams(vmem_limit_bytes=48 * 1024 * 1024),
    )(template, mine, partner, first_table, second_half, twiddle_cos, twiddle_sin, *gates, row0)


def per_device(strain, bank, owners, gate_start, gate_width):
    count_a = strain.shape[2]
    count_b = strain.shape[3]
    block_count = owners.shape[1]
    half_rows = count_b // 2
    first_table = dft_table(count_a)
    second_table = dft_table(count_b)
    twiddle_cos, twiddle_sin = twiddle(count_a, count_b)
    first_table, second_table, twiddle_cos, twiddle_sin = lax.optimization_barrier(
        (first_table, second_table, twiddle_cos, twiddle_sin)
    )
    series = strain[0]
    stored = bank[0]
    detector_side = lax.axis_index("z") % 2
    row_start = detector_side * half_rows
    partner_series, partner_start, partner_width = [
        from_partner(block, "z", 0) for block in (series, gate_start[0], gate_width[0])
    ]
    gates = (gate_start[0], gate_width[0], partner_start, partner_width)
    second_half = jnp.concatenate(
        [
            lax.dynamic_slice_in_dim(second_table, row_start, half_rows, 0),
            lax.dynamic_slice_in_dim(second_table, count_b + row_start, half_rows, 0),
        ]
    )
    row0 = jnp.reshape(row_start, (1,)).astype(jnp.int32)
    own_tmpl, other_tmpl, side, partner_series, gates = spread(
        stored, owners[0], "xlo", "z", partner_series, gates
    )
    networks = []
    for template in (own_tmpl, other_tmpl):
        if networks:
            template, _ = lax.optimization_barrier((template, networks[-1]))
        networks.append(
            network_call(
                template,
                series,
                partner_series,
                first_table,
                second_half,
                twiddle_cos,
                twiddle_sin,
                gates,
                row0,
            )
        )
    loudest = butterfly_max(jnp.maximum(networks[0], networks[1]), "tmpl")
    network = jnp.where(
        side == 0, jnp.stack([networks[0], networks[1]]), jnp.stack([networks[1], networks[0]])
    )
    network = network.reshape(block_count, 1, half_rows * count_a)
    loudest = loudest.reshape(1, half_rows * count_a)
    return (network, loudest)


def solution(mesh):
    tmpl_count = mesh.shape["tmpl"]
    seg_count = mesh.shape["seg"]
    grid = Mesh(mesh.devices.reshape(tmpl_count, 2, seg_count // 2), ("tmpl", "xlo", "z"))
    seg = ("xlo", "z")
    in_specs = (
        P(seg, None, None, None),
        P(("tmpl",) + seg, None, None, None),
        P("tmpl", None),
        P(seg, None),
        P(seg, None),
    )
    out_specs = (P("tmpl", seg, None), P(seg, None))
    return jax.shard_map(
        per_device, mesh=grid, in_specs=in_specs, out_specs=out_specs, check_vma=False
    )
```

```python
import math

import jax
import jax.numpy as jnp
from jax import lax
from jax.experimental import pallas as pl
from jax.experimental.pallas import tpu as pltpu
from jax.sharding import Mesh
from jax.sharding import PartitionSpec as P


def spread(stored, owners, row_axis, ring_axis):
    ring = lax.axis_size(ring_axis)
    row = lax.axis_index(row_axis)
    spot = lax.axis_index(ring_axis)
    width = stored.shape[-1]
    chunks = stored.reshape(ring, -1, width)
    bits = ring.bit_length() - 1
    order = [sum(((place >> bit) & 1) << (bits - 1 - bit) for bit in range(bits)) for place in range(ring)]
    outgoing = chunks[jnp.array(order)].reshape(-1, width)
    incoming = lax.all_to_all(outgoing, ring_axis, 0, 0, tiled=True).reshape(ring, -1, width)
    own_holder = jnp.where(row == 0, owners[0], owners[1])
    other_holder = jnp.where(row == 0, owners[1], owners[0])
    mine = lax.dynamic_index_in_dim(incoming, own_holder % ring, 0, keepdims=False)
    theirs = lax.dynamic_index_in_dim(incoming, other_holder % ring, 0, keepdims=False)
    swap = [(0, 1), (1, 0)]
    got = lax.ppermute(theirs, row_axis, swap)
    flat = jnp.where(own_holder // ring == row, mine, got)
    apart = ring // 2
    while apart >= 1:
        side = (spot // apart) % 2
        route = [(low, low ^ apart) for low in range(ring)]
        if apart == 1:
            early = lax.ppermute(flat, row_axis, swap)
        other = lax.ppermute(flat, ring_axis, route)
        if apart == 1:
            late = lax.ppermute(other, row_axis, swap)
            theirs = jnp.where(
                side == 0,
                jnp.concatenate([early, late], axis=0),
                jnp.concatenate([late, early], axis=0),
            )
        flat = jnp.where(
            side == 0,
            jnp.concatenate([flat, other], axis=0),
            jnp.concatenate([other, flat], axis=0),
        )
        apart //= 2
    return flat.reshape(stored.shape), theirs.reshape(stored.shape), row


def butterfly_max(block, axis):
    count = lax.axis_size(axis)
    apart = count // 2
    while apart >= 1:
        route = [(low, low ^ apart) for low in range(count)]
        block = jnp.maximum(block, lax.ppermute(block, axis, route))
        apart //= 2
    return block


def from_partner(block, axis, apart):
    count = lax.axis_size(axis)
    route = []
    for low in range(count):
        high = low | 1 << apart
        if high != low and high < count:
            route += [(low, high), (high, low)]
    return lax.ppermute(block, axis, route)


def dft_table(length):
    positions = jnp.arange(length, dtype=jnp.int32)
    angles = (positions[:, None] * positions[None, :] % length).astype(jnp.float32) * (
        2.0 * math.pi / length
    )
    return jnp.concatenate([jnp.cos(angles), jnp.sin(angles)], axis=0).astype(jnp.bfloat16)


def twiddle(row_count, col_count):
    row_index = jnp.arange(row_count, dtype=jnp.int32)[:, None]
    col_index = jnp.arange(col_count, dtype=jnp.int32)[None, :]
    angles = (row_index * col_index % (row_count * col_count)).astype(jnp.float32) * (
        2.0 * math.pi / (row_count * col_count)
    )
    return (jnp.cos(angles), jnp.sin(angles))


def gate_mask(starts, widths, row_count, col_count):
    moment = (
        jnp.arange(row_count, dtype=jnp.int32)[:, None] * col_count
        + jnp.arange(col_count, dtype=jnp.int32)[None, :]
    )
    flags = jnp.zeros((row_count, col_count), dtype=jnp.bool_)
    for number in range(starts.shape[0]):
        flags = flags | (moment >= starts[number]) & (moment < starts[number] + widths[number])
    return flags


def filter_power(template, series, flags, first_table, second_table, twiddle_cos, twiddle_sin):
    count_a = template.shape[1]
    count_b = template.shape[2]
    out_rows = second_table.shape[0] // 2
    tmpl_re = template[0].astype(jnp.float32)
    tmpl_im = template[1].astype(jnp.float32)
    data_re = series[0].astype(jnp.float32)
    data_im = series[1].astype(jnp.float32)
    prod_re = data_re * tmpl_re + data_im * tmpl_im
    prod_im = data_im * tmpl_re - data_re * tmpl_im
    joined = jnp.concatenate([prod_re, prod_im], axis=1).astype(jnp.bfloat16)
    section_one = jnp.dot(first_table, joined, preferred_element_type=jnp.float32)
    section_re = section_one[:count_a, :count_b] - section_one[count_a:, count_b:]
    section_im = section_one[:count_a, count_b:] + section_one[count_a:, :count_b]
    turned = jnp.concatenate(
        [
            section_re * twiddle_cos - section_im * twiddle_sin,
            section_re * twiddle_sin + section_im * twiddle_cos,
        ],
        axis=0,
    ).astype(jnp.bfloat16)
    section_two = lax.dot_general(
        second_table, turned, (((1,), (1,)), ((), ())), preferred_element_type=jnp.float32
    )
    snr_re = section_two[:out_rows, :count_a] - section_two[out_rows:, count_a:]
    snr_im = section_two[:out_rows, count_a:] + section_two[out_rows:, :count_a]
    norm_sq = jnp.sum(tmpl_re * tmpl_re + tmpl_im * tmpl_im) + 1e-06
    snr_power = (snr_re * snr_re + snr_im * snr_im) / norm_sq
    return jnp.where(flags, 0.0, snr_power).astype(jnp.bfloat16)


def filter_kernel(
    template_ref, series_ref, first_ref, second_ref, cos_ref, sin_ref, start_ref, width_ref, out_ref
):
    count_a = template_ref.shape[1]
    count_b = template_ref.shape[2]
    out_rows = second_ref.shape[0] // 2
    tmpl_re = template_ref[0].astype(jnp.float32)
    tmpl_im = template_ref[1].astype(jnp.float32)
    data_re = series_ref[0].astype(jnp.float32)
    data_im = series_ref[1].astype(jnp.float32)
    prod_re = (data_re * tmpl_re + data_im * tmpl_im).astype(jnp.bfloat16)
    prod_im = (data_im * tmpl_re - data_re * tmpl_im).astype(jnp.bfloat16)
    first = first_ref[...]
    left = jnp.dot(first, prod_re, preferred_element_type=jnp.float32)
    right = jnp.dot(first, prod_im, preferred_element_type=jnp.float32)
    section_re = left[:count_a] - right[count_a:]
    section_im = right[:count_a] + left[count_a:]
    turn_cos = cos_ref[...]
    turn_sin = sin_ref[...]
    turned_re = (section_re * turn_cos - section_im * turn_sin).astype(jnp.bfloat16)
    turned_im = (section_re * turn_sin + section_im * turn_cos).astype(jnp.bfloat16)
    second = second_ref[...]
    contract = (((1,), (1,)), ((), ()))
    left = lax.dot_general(second, turned_re, contract, preferred_element_type=jnp.float32)
    right = lax.dot_general(second, turned_im, contract, preferred_element_type=jnp.float32)
    snr_re = left[:out_rows] - right[out_rows:]
    snr_im = right[:out_rows] + left[out_rows:]
    norm_sq = jnp.sum(tmpl_re * tmpl_re + tmpl_im * tmpl_im) + 1e-06
    snr_power = (snr_re * snr_re + snr_im * snr_im) / norm_sq
    moment = (
        lax.broadcasted_iota(jnp.int32, snr_power.shape, 0) * count_a
        + lax.broadcasted_iota(jnp.int32, snr_power.shape, 1)
    )
    flags = jnp.zeros(snr_power.shape, dtype=jnp.bool_)
    for number in range(start_ref.shape[0]):
        begin = start_ref[number]
        flags = flags | (moment >= begin) & (moment < begin + width_ref[number])
    out_ref[...] = jnp.where(flags, 0.0, snr_power).astype(jnp.bfloat16)


def filter_call(template, series, first_table, second_table, twiddle_cos, twiddle_sin, starts, widths):
    vmem = pltpu.MemorySpace.VMEM
    smem = pltpu.MemorySpace.SMEM
    rows = second_table.shape[0] // 2
    return pl.pallas_call(
        filter_kernel,
        out_shape=jax.ShapeDtypeStruct((rows, template.shape[1]), jnp.bfloat16),
        in_specs=[pl.BlockSpec(memory_space=vmem)] * 6 + [pl.BlockSpec(memory_space=smem)] * 2,
        out_specs=pl.BlockSpec(memory_space=vmem),
        compiler_params=pltpu.CompilerParams(vmem_limit_bytes=48 * 1024 * 1024),
    )(template, series, first_table, second_table, twiddle_cos, twiddle_sin, starts, widths)


def per_device(strain, bank, owners, gate_start, gate_width):
    count_a = strain.shape[2]
    count_b = strain.shape[3]
    block_count = owners.shape[1]
    half_rows = count_b // 2
    first_table = dft_table(count_a)
    second_table = dft_table(count_b)
    twiddle_cos, twiddle_sin = twiddle(count_a, count_b)
    first_table, second_table, twiddle_cos, twiddle_sin = lax.optimization_barrier(
        (first_table, second_table, twiddle_cos, twiddle_sin)
    )
    series = strain[0]
    stored = bank[0]
    detector_side = lax.axis_index("z") % 2
    row_start = detector_side * half_rows
    own_tmpl, other_tmpl, side = spread(stored, owners[0], "xlo", "z")
    networks = []
    power = None
    for template in (own_tmpl, other_tmpl):
        if power is not None:
            template, power = lax.optimization_barrier((template, power))
        power = filter_call(
            template,
            series,
            first_table,
            second_table,
            twiddle_cos,
            twiddle_sin,
            gate_start[0],
            gate_width[0],
        )
        own_half = lax.dynamic_slice_in_dim(power, row_start, half_rows, 0)
        other_half = lax.dynamic_slice_in_dim(power, half_rows - row_start, half_rows, 0)
        partner = from_partner(other_half, "z", 0)
        networks.append(
            jnp.sqrt(own_half.astype(jnp.float32) + partner.astype(jnp.float32)).astype(
                jnp.bfloat16
            )
        )
    loudest = butterfly_max(jnp.maximum(networks[0], networks[1]), "tmpl")
    network = jnp.where(
        side == 0, jnp.stack([networks[0], networks[1]]), jnp.stack([networks[1], networks[0]])
    )
    network = network.reshape(block_count, 1, half_rows * count_a)
    loudest = loudest.reshape(1, half_rows * count_a)
    return (network, loudest)


def solution(mesh):
    tmpl_count = mesh.shape["tmpl"]
    seg_count = mesh.shape["seg"]
    grid = Mesh(mesh.devices.reshape(tmpl_count, 2, seg_count // 2), ("tmpl", "xlo", "z"))
    seg = ("xlo", "z")
    in_specs = (
        P(seg, None, None, None),
        P(("tmpl",) + seg, None, None, None),
        P("tmpl", None),
        P(seg, None),
        P(seg, None),
    )
    out_specs = (P("tmpl", seg, None), P(seg, None))
    return jax.shard_map(
        per_device, mesh=grid, in_specs=in_specs, out_specs=out_specs, check_vma=False
    )
```

```python
import math

import jax
import jax.numpy as jnp
from jax import lax
from jax.experimental import pallas as pl
from jax.experimental.pallas import tpu as pltpu
from jax.sharding import Mesh
from jax.sharding import PartitionSpec as P


def spread(stored, owners, row_axis, ring_axis, riders):
    ring = lax.axis_size(ring_axis)
    row = lax.axis_index(row_axis)
    spot = lax.axis_index(ring_axis)
    width = stored.shape[-1]
    chunks = stored.reshape(ring, -1, width)
    bits = ring.bit_length() - 1
    order = [sum(((place >> bit) & 1) << (bits - 1 - bit) for bit in range(bits)) for place in range(ring)]
    outgoing = chunks[jnp.array(order)].reshape(-1, width)
    incoming = lax.all_to_all(outgoing, ring_axis, 0, 0, tiled=True).reshape(ring, -1, width)
    own_holder = jnp.where(row == 0, owners[0], owners[1])
    other_holder = jnp.where(row == 0, owners[1], owners[0])
    mine = lax.dynamic_index_in_dim(incoming, own_holder % ring, 0, keepdims=False)
    theirs = lax.dynamic_index_in_dim(incoming, other_holder % ring, 0, keepdims=False)
    swap = [(0, 1), (1, 0)]
    got = lax.ppermute(theirs, row_axis, swap)
    flat = jnp.where(own_holder // ring == row, mine, got)
    flat, riders = lax.optimization_barrier((flat, riders))
    apart = ring // 2
    while apart >= 1:
        side = (spot // apart) % 2
        route = [(low, low ^ apart) for low in range(ring)]
        if apart == 1:
            early = lax.ppermute(flat, row_axis, swap)
        other = lax.ppermute(flat, ring_axis, route)
        if apart == 1:
            late = lax.ppermute(other, row_axis, swap)
            theirs = jnp.where(
                side == 0,
                jnp.concatenate([early, late], axis=0),
                jnp.concatenate([late, early], axis=0),
            )
        flat = jnp.where(
            side == 0,
            jnp.concatenate([flat, other], axis=0),
            jnp.concatenate([other, flat], axis=0),
        )
        apart //= 2
    return flat.reshape(stored.shape), theirs.reshape(stored.shape), row, riders


def butterfly_max(block, axis):
    count = lax.axis_size(axis)
    apart = count // 2
    while apart >= 1:
        route = [(low, low ^ apart) for low in range(count)]
        block = jnp.maximum(block, lax.ppermute(block, axis, route))
        apart //= 2
    return block


def from_partner(block, axis, apart):
    count = lax.axis_size(axis)
    route = []
    for low in range(count):
        high = low | 1 << apart
        if high != low and high < count:
            route += [(low, high), (high, low)]
    return lax.ppermute(block, axis, route)


def dft_table(length):
    positions = jnp.arange(length, dtype=jnp.int32)
    angles = (positions[:, None] * positions[None, :] % length).astype(jnp.float32) * (
        2.0 * math.pi / length
    )
    return jnp.concatenate([jnp.cos(angles), jnp.sin(angles)], axis=0).astype(jnp.bfloat16)


def twiddle(row_count, col_count):
    row_index = jnp.arange(row_count, dtype=jnp.int32)[:, None]
    col_index = jnp.arange(col_count, dtype=jnp.int32)[None, :]
    angles = (row_index * col_index % (row_count * col_count)).astype(jnp.float32) * (
        2.0 * math.pi / (row_count * col_count)
    )
    return (jnp.cos(angles), jnp.sin(angles))


def gate_mask(starts, widths, row_count, col_count):
    moment = (
        jnp.arange(row_count, dtype=jnp.int32)[:, None] * col_count
        + jnp.arange(col_count, dtype=jnp.int32)[None, :]
    )
    flags = jnp.zeros((row_count, col_count), dtype=jnp.bool_)
    for number in range(starts.shape[0]):
        flags = flags | (moment >= starts[number]) & (moment < starts[number] + widths[number])
    return flags


def filter_power(template, series, flags, first_table, second_table, twiddle_cos, twiddle_sin):
    count_a = template.shape[1]
    count_b = template.shape[2]
    out_rows = second_table.shape[0] // 2
    tmpl_re = template[0].astype(jnp.float32)
    tmpl_im = template[1].astype(jnp.float32)
    data_re = series[0].astype(jnp.float32)
    data_im = series[1].astype(jnp.float32)
    prod_re = data_re * tmpl_re + data_im * tmpl_im
    prod_im = data_im * tmpl_re - data_re * tmpl_im
    joined = jnp.concatenate([prod_re, prod_im], axis=1).astype(jnp.bfloat16)
    section_one = jnp.dot(first_table, joined, preferred_element_type=jnp.float32)
    section_re = section_one[:count_a, :count_b] - section_one[count_a:, count_b:]
    section_im = section_one[:count_a, count_b:] + section_one[count_a:, :count_b]
    turned = jnp.concatenate(
        [
            section_re * twiddle_cos - section_im * twiddle_sin,
            section_re * twiddle_sin + section_im * twiddle_cos,
        ],
        axis=0,
    ).astype(jnp.bfloat16)
    section_two = lax.dot_general(
        second_table, turned, (((1,), (1,)), ((), ())), preferred_element_type=jnp.float32
    )
    snr_re = section_two[:out_rows, :count_a] - section_two[out_rows:, count_a:]
    snr_im = section_two[:out_rows, count_a:] + section_two[out_rows:, :count_a]
    norm_sq = jnp.sum(tmpl_re * tmpl_re + tmpl_im * tmpl_im) + 1e-06
    snr_power = (snr_re * snr_re + snr_im * snr_im) / norm_sq
    return jnp.where(flags, 0.0, snr_power).astype(jnp.bfloat16)


def filter_kernel(
    template_ref, series_ref, first_ref, second_ref, cos_ref, sin_ref, start_ref, width_ref, out_ref
):
    count_a = template_ref.shape[1]
    count_b = template_ref.shape[2]
    out_rows = second_ref.shape[0] // 2
    tmpl_re = template_ref[0].astype(jnp.float32)
    tmpl_im = template_ref[1].astype(jnp.float32)
    data_re = series_ref[0].astype(jnp.float32)
    data_im = series_ref[1].astype(jnp.float32)
    prod_re = (data_re * tmpl_re + data_im * tmpl_im).astype(jnp.bfloat16)
    prod_im = (data_im * tmpl_re - data_re * tmpl_im).astype(jnp.bfloat16)
    first = first_ref[...]
    left = jnp.dot(first, prod_re, preferred_element_type=jnp.float32)
    right = jnp.dot(first, prod_im, preferred_element_type=jnp.float32)
    section_re = left[:count_a] - right[count_a:]
    section_im = right[:count_a] + left[count_a:]
    turn_cos = cos_ref[...]
    turn_sin = sin_ref[...]
    turned_re = (section_re * turn_cos - section_im * turn_sin).astype(jnp.bfloat16)
    turned_im = (section_re * turn_sin + section_im * turn_cos).astype(jnp.bfloat16)
    second = second_ref[...]
    contract = (((1,), (1,)), ((), ()))
    left = lax.dot_general(second, turned_re, contract, preferred_element_type=jnp.float32)
    right = lax.dot_general(second, turned_im, contract, preferred_element_type=jnp.float32)
    snr_re = left[:out_rows] - right[out_rows:]
    snr_im = right[:out_rows] + left[out_rows:]
    norm_sq = jnp.sum(tmpl_re * tmpl_re + tmpl_im * tmpl_im) + 1e-06
    snr_power = (snr_re * snr_re + snr_im * snr_im) / norm_sq
    moment = (
        lax.broadcasted_iota(jnp.int32, snr_power.shape, 0) * count_a
        + lax.broadcasted_iota(jnp.int32, snr_power.shape, 1)
    )
    flags = jnp.zeros(snr_power.shape, dtype=jnp.bool_)
    for number in range(start_ref.shape[0]):
        begin = start_ref[number]
        flags = flags | (moment >= begin) & (moment < begin + width_ref[number])
    out_ref[...] = jnp.where(flags, 0.0, snr_power).astype(jnp.bfloat16)


def filter_call(template, series, first_table, second_table, twiddle_cos, twiddle_sin, starts, widths):
    vmem = pltpu.MemorySpace.VMEM
    smem = pltpu.MemorySpace.SMEM
    rows = second_table.shape[0] // 2
    return pl.pallas_call(
        filter_kernel,
        out_shape=jax.ShapeDtypeStruct((rows, template.shape[1]), jnp.bfloat16),
        in_specs=[pl.BlockSpec(memory_space=vmem)] * 6 + [pl.BlockSpec(memory_space=smem)] * 2,
        out_specs=pl.BlockSpec(memory_space=vmem),
        compiler_params=pltpu.CompilerParams(vmem_limit_bytes=48 * 1024 * 1024),
    )(template, series, first_table, second_table, twiddle_cos, twiddle_sin, starts, widths)


def per_device(strain, bank, owners, gate_start, gate_width):
    count_a = strain.shape[2]
    count_b = strain.shape[3]
    block_count = owners.shape[1]
    half_rows = count_b // 2
    first_table = dft_table(count_a)
    second_table = dft_table(count_b)
    twiddle_cos, twiddle_sin = twiddle(count_a, count_b)
    series = strain[0]
    stored = bank[0]
    detector_side = lax.axis_index("z") % 2
    row_start = detector_side * half_rows
    own_tmpl, other_tmpl, side, tables = spread(
        stored, owners[0], "xlo", "z", (first_table, second_table, twiddle_cos, twiddle_sin)
    )
    first_table, second_table, twiddle_cos, twiddle_sin = tables
    networks = []
    power = None
    for template in (own_tmpl, other_tmpl):
        if power is not None:
            template, power = lax.optimization_barrier((template, power))
        power = filter_call(
            template,
            series,
            first_table,
            second_table,
            twiddle_cos,
            twiddle_sin,
            gate_start[0],
            gate_width[0],
        )
        own_half = lax.dynamic_slice_in_dim(power, row_start, half_rows, 0)
        other_half = lax.dynamic_slice_in_dim(power, half_rows - row_start, half_rows, 0)
        partner = from_partner(other_half, "z", 0)
        networks.append(
            jnp.sqrt(own_half.astype(jnp.float32) + partner.astype(jnp.float32)).astype(
                jnp.bfloat16
            )
        )
    loudest = butterfly_max(jnp.maximum(networks[0], networks[1]), "tmpl")
    network = jnp.where(
        side == 0, jnp.stack([networks[0], networks[1]]), jnp.stack([networks[1], networks[0]])
    )
    network = network.reshape(block_count, 1, half_rows * count_a)
    loudest = loudest.reshape(1, half_rows * count_a)
    return (network, loudest)


def solution(mesh):
    tmpl_count = mesh.shape["tmpl"]
    seg_count = mesh.shape["seg"]
    grid = Mesh(mesh.devices.reshape(tmpl_count, 2, seg_count // 2), ("tmpl", "xlo", "z"))
    seg = ("xlo", "z")
    in_specs = (
        P(seg, None, None, None),
        P(("tmpl",) + seg, None, None, None),
        P("tmpl", None),
        P(seg, None),
        P(seg, None),
    )
    out_specs = (P("tmpl", seg, None), P(seg, None))
    return jax.shard_map(
        per_device, mesh=grid, in_specs=in_specs, out_specs=out_specs, check_vma=False
    )
```

```python
import math

import jax
import jax.numpy as jnp
from jax import lax
from jax.experimental import pallas as pl
from jax.experimental.pallas import tpu as pltpu
from jax.sharding import Mesh
from jax.sharding import PartitionSpec as P


def spread(stored, owners, row_axis, ring_axis, riders):
    ring = lax.axis_size(ring_axis)
    row = lax.axis_index(row_axis)
    spot = lax.axis_index(ring_axis)
    width = stored.shape[-1]
    chunks = stored.reshape(ring, -1, width)
    bits = ring.bit_length() - 1
    order = [sum(((place >> bit) & 1) << (bits - 1 - bit) for bit in range(bits)) for place in range(ring)]
    outgoing = chunks[jnp.array(order)].reshape(-1, width)
    incoming = lax.all_to_all(outgoing, ring_axis, 0, 0, tiled=True).reshape(ring, -1, width)
    own_holder = jnp.where(row == 0, owners[0], owners[1])
    other_holder = jnp.where(row == 0, owners[1], owners[0])
    mine = lax.dynamic_index_in_dim(incoming, own_holder % ring, 0, keepdims=False)
    theirs = lax.dynamic_index_in_dim(incoming, other_holder % ring, 0, keepdims=False)
    swap = [(0, 1), (1, 0)]
    got = lax.ppermute(theirs, row_axis, swap)
    flat = jnp.where(own_holder // ring == row, mine, got)
    flat, riders = lax.optimization_barrier((flat, riders))
    apart = ring // 2
    while apart >= 1:
        side = (spot // apart) % 2
        route = [(low, low ^ apart) for low in range(ring)]
        if apart == 1:
            early = lax.ppermute(flat, row_axis, swap)
        other = lax.ppermute(flat, ring_axis, route)
        if apart == 1:
            both = (row_axis, ring_axis)
            across = [(low, low ^ ring ^ 1) for low in range(2 * ring)]
            late = lax.ppermute(flat, both, across)
            theirs = jnp.where(
                side == 0,
                jnp.concatenate([early, late], axis=0),
                jnp.concatenate([late, early], axis=0),
            )
        flat = jnp.where(
            side == 0,
            jnp.concatenate([flat, other], axis=0),
            jnp.concatenate([other, flat], axis=0),
        )
        apart //= 2
    return flat.reshape(stored.shape), theirs.reshape(stored.shape), row, riders


def butterfly_max(block, axis):
    count = lax.axis_size(axis)
    apart = count // 2
    while apart >= 1:
        route = [(low, low ^ apart) for low in range(count)]
        block = jnp.maximum(block, lax.ppermute(block, axis, route))
        apart //= 2
    return block


def from_partner(block, axis, apart):
    count = lax.axis_size(axis)
    route = []
    for low in range(count):
        high = low | 1 << apart
        if high != low and high < count:
            route += [(low, high), (high, low)]
    return lax.ppermute(block, axis, route)


def dft_table(length):
    positions = jnp.arange(length, dtype=jnp.int32)
    angles = (positions[:, None] * positions[None, :] % length).astype(jnp.float32) * (
        2.0 * math.pi / length
    )
    return jnp.concatenate([jnp.cos(angles), jnp.sin(angles)], axis=0).astype(jnp.bfloat16)


def twiddle(row_count, col_count):
    row_index = jnp.arange(row_count, dtype=jnp.int32)[:, None]
    col_index = jnp.arange(col_count, dtype=jnp.int32)[None, :]
    angles = (row_index * col_index % (row_count * col_count)).astype(jnp.float32) * (
        2.0 * math.pi / (row_count * col_count)
    )
    return (jnp.cos(angles), jnp.sin(angles))


def gate_mask(starts, widths, row_count, col_count):
    moment = (
        jnp.arange(row_count, dtype=jnp.int32)[:, None] * col_count
        + jnp.arange(col_count, dtype=jnp.int32)[None, :]
    )
    flags = jnp.zeros((row_count, col_count), dtype=jnp.bool_)
    for number in range(starts.shape[0]):
        flags = flags | (moment >= starts[number]) & (moment < starts[number] + widths[number])
    return flags


def filter_power(template, series, flags, first_table, second_table, twiddle_cos, twiddle_sin):
    count_a = template.shape[1]
    count_b = template.shape[2]
    out_rows = second_table.shape[0] // 2
    tmpl_re = template[0].astype(jnp.float32)
    tmpl_im = template[1].astype(jnp.float32)
    data_re = series[0].astype(jnp.float32)
    data_im = series[1].astype(jnp.float32)
    prod_re = data_re * tmpl_re + data_im * tmpl_im
    prod_im = data_im * tmpl_re - data_re * tmpl_im
    joined = jnp.concatenate([prod_re, prod_im], axis=1).astype(jnp.bfloat16)
    section_one = jnp.dot(first_table, joined, preferred_element_type=jnp.float32)
    section_re = section_one[:count_a, :count_b] - section_one[count_a:, count_b:]
    section_im = section_one[:count_a, count_b:] + section_one[count_a:, :count_b]
    turned = jnp.concatenate(
        [
            section_re * twiddle_cos - section_im * twiddle_sin,
            section_re * twiddle_sin + section_im * twiddle_cos,
        ],
        axis=0,
    ).astype(jnp.bfloat16)
    section_two = lax.dot_general(
        second_table, turned, (((1,), (1,)), ((), ())), preferred_element_type=jnp.float32
    )
    snr_re = section_two[:out_rows, :count_a] - section_two[out_rows:, count_a:]
    snr_im = section_two[:out_rows, count_a:] + section_two[out_rows:, :count_a]
    norm_sq = jnp.sum(tmpl_re * tmpl_re + tmpl_im * tmpl_im) + 1e-06
    snr_power = (snr_re * snr_re + snr_im * snr_im) / norm_sq
    return jnp.where(flags, 0.0, snr_power).astype(jnp.bfloat16)


def filter_kernel(
    template_ref, series_ref, first_ref, second_ref, cos_ref, sin_ref, start_ref, width_ref, out_ref
):
    count_a = template_ref.shape[1]
    count_b = template_ref.shape[2]
    out_rows = second_ref.shape[0] // 2
    tmpl_re = template_ref[0].astype(jnp.float32)
    tmpl_im = template_ref[1].astype(jnp.float32)
    data_re = series_ref[0].astype(jnp.float32)
    data_im = series_ref[1].astype(jnp.float32)
    prod_re = (data_re * tmpl_re + data_im * tmpl_im).astype(jnp.bfloat16)
    prod_im = (data_im * tmpl_re - data_re * tmpl_im).astype(jnp.bfloat16)
    first = first_ref[...]
    left = jnp.dot(first, prod_re, preferred_element_type=jnp.float32)
    right = jnp.dot(first, prod_im, preferred_element_type=jnp.float32)
    section_re = left[:count_a] - right[count_a:]
    section_im = right[:count_a] + left[count_a:]
    turn_cos = cos_ref[...]
    turn_sin = sin_ref[...]
    turned_re = (section_re * turn_cos - section_im * turn_sin).astype(jnp.bfloat16)
    turned_im = (section_re * turn_sin + section_im * turn_cos).astype(jnp.bfloat16)
    second = second_ref[...]
    contract = (((1,), (1,)), ((), ()))
    left = lax.dot_general(second, turned_re, contract, preferred_element_type=jnp.float32)
    right = lax.dot_general(second, turned_im, contract, preferred_element_type=jnp.float32)
    snr_re = left[:out_rows] - right[out_rows:]
    snr_im = right[:out_rows] + left[out_rows:]
    norm_sq = jnp.sum(tmpl_re * tmpl_re + tmpl_im * tmpl_im) + 1e-06
    snr_power = (snr_re * snr_re + snr_im * snr_im) / norm_sq
    moment = (
        lax.broadcasted_iota(jnp.int32, snr_power.shape, 0) * count_a
        + lax.broadcasted_iota(jnp.int32, snr_power.shape, 1)
    )
    flags = jnp.zeros(snr_power.shape, dtype=jnp.bool_)
    for number in range(start_ref.shape[0]):
        begin = start_ref[number]
        flags = flags | (moment >= begin) & (moment < begin + width_ref[number])
    out_ref[...] = jnp.where(flags, 0.0, snr_power).astype(jnp.bfloat16)


def filter_call(template, series, first_table, second_table, twiddle_cos, twiddle_sin, starts, widths):
    vmem = pltpu.MemorySpace.VMEM
    smem = pltpu.MemorySpace.SMEM
    rows = second_table.shape[0] // 2
    return pl.pallas_call(
        filter_kernel,
        out_shape=jax.ShapeDtypeStruct((rows, template.shape[1]), jnp.bfloat16),
        in_specs=[pl.BlockSpec(memory_space=vmem)] * 6 + [pl.BlockSpec(memory_space=smem)] * 2,
        out_specs=pl.BlockSpec(memory_space=vmem),
        compiler_params=pltpu.CompilerParams(vmem_limit_bytes=48 * 1024 * 1024),
    )(template, series, first_table, second_table, twiddle_cos, twiddle_sin, starts, widths)


def per_device(strain, bank, owners, gate_start, gate_width):
    count_a = strain.shape[2]
    count_b = strain.shape[3]
    block_count = owners.shape[1]
    half_rows = count_b // 2
    first_table = dft_table(count_a)
    second_table = dft_table(count_b)
    twiddle_cos, twiddle_sin = twiddle(count_a, count_b)
    series = strain[0]
    stored = bank[0]
    detector_side = lax.axis_index("z") % 2
    row_start = detector_side * half_rows
    own_tmpl, other_tmpl, side, tables = spread(
        stored, owners[0], "xlo", "z", (first_table, second_table, twiddle_cos, twiddle_sin)
    )
    first_table, second_table, twiddle_cos, twiddle_sin = tables
    networks = []
    power = None
    for template in (own_tmpl, other_tmpl):
        if power is not None:
            template, power = lax.optimization_barrier((template, power))
        power = filter_call(
            template,
            series,
            first_table,
            second_table,
            twiddle_cos,
            twiddle_sin,
            gate_start[0],
            gate_width[0],
        )
        own_half = lax.dynamic_slice_in_dim(power, row_start, half_rows, 0)
        other_half = lax.dynamic_slice_in_dim(power, half_rows - row_start, half_rows, 0)
        partner = from_partner(other_half, "z", 0)
        networks.append(
            jnp.sqrt(own_half.astype(jnp.float32) + partner.astype(jnp.float32)).astype(
                jnp.bfloat16
            )
        )
    loudest = butterfly_max(jnp.maximum(networks[0], networks[1]), "tmpl")
    network = jnp.where(
        side == 0, jnp.stack([networks[0], networks[1]]), jnp.stack([networks[1], networks[0]])
    )
    network = network.reshape(block_count, 1, half_rows * count_a)
    loudest = loudest.reshape(1, half_rows * count_a)
    return (network, loudest)


def solution(mesh):
    tmpl_count = mesh.shape["tmpl"]
    seg_count = mesh.shape["seg"]
    grid = Mesh(mesh.devices.reshape(tmpl_count, 2, seg_count // 2), ("tmpl", "xlo", "z"))
    seg = ("xlo", "z")
    in_specs = (
        P(seg, None, None, None),
        P(("tmpl",) + seg, None, None, None),
        P("tmpl", None),
        P(seg, None),
        P(seg, None),
    )
    out_specs = (P("tmpl", seg, None), P(seg, None))
    return jax.shard_map(
        per_device, mesh=grid, in_specs=in_specs, out_specs=out_specs, check_vma=False
    )
```

```python
import math

import jax
import jax.numpy as jnp
from jax import lax
from jax.experimental import pallas as pl
from jax.experimental.pallas import tpu as pltpu
from jax.sharding import Mesh
from jax.sharding import PartitionSpec as P


def spread(stored, owners, row_axis, ring_axis, riders, early):
    ring = lax.axis_size(ring_axis)
    row = lax.axis_index(row_axis)
    spot = lax.axis_index(ring_axis)
    width = stored.shape[-1]
    chunks = stored.reshape(ring, -1, width)
    bits = ring.bit_length() - 1
    order = [sum(((place >> bit) & 1) << (bits - 1 - bit) for bit in range(bits)) for place in range(ring)]
    outgoing = chunks[jnp.array(order)].reshape(-1, width)
    incoming = lax.all_to_all(outgoing, ring_axis, 0, 0, tiled=True).reshape(ring, -1, width)
    incoming, early, riders = lax.optimization_barrier((incoming, early, riders))
    riders = lax.ppermute(riders, ring_axis, [(low, low ^ 1) for low in range(ring)])
    own_holder = jnp.where(row == 0, owners[0], owners[1])
    other_holder = jnp.where(row == 0, owners[1], owners[0])
    mine = lax.dynamic_index_in_dim(incoming, own_holder % ring, 0, keepdims=False)
    theirs = lax.dynamic_index_in_dim(incoming, other_holder % ring, 0, keepdims=False)
    swap = [(0, 1), (1, 0)]
    got = lax.ppermute(theirs, row_axis, swap)
    flat = jnp.where(own_holder // ring == row, mine, got)
    apart = ring // 2
    while apart >= 1:
        side = (spot // apart) % 2
        route = [(low, low ^ apart) for low in range(ring)]
        if apart == 1:
            flat, riders = lax.optimization_barrier((flat, riders))
            ahead = lax.ppermute(flat, row_axis, swap)
        other = lax.ppermute(flat, ring_axis, route)
        if apart == 1:
            late = lax.ppermute(other, row_axis, swap)
            theirs = jnp.where(
                side == 0,
                jnp.concatenate([ahead, late], axis=0),
                jnp.concatenate([late, ahead], axis=0),
            )
        flat = jnp.where(
            side == 0,
            jnp.concatenate([flat, other], axis=0),
            jnp.concatenate([other, flat], axis=0),
        )
        apart //= 2
    return flat.reshape(stored.shape), theirs.reshape(stored.shape), row, riders, early


def butterfly_max(block, axis):
    count = lax.axis_size(axis)
    apart = count // 2
    while apart >= 1:
        route = [(low, low ^ apart) for low in range(count)]
        block = jnp.maximum(block, lax.ppermute(block, axis, route))
        apart //= 2
    return block


def from_partner(block, axis, apart):
    count = lax.axis_size(axis)
    route = []
    for low in range(count):
        high = low | 1 << apart
        if high != low and high < count:
            route += [(low, high), (high, low)]
    return lax.ppermute(block, axis, route)


def dft_table(length):
    positions = jnp.arange(length, dtype=jnp.int32)
    angles = (positions[:, None] * positions[None, :] % length).astype(jnp.float32) * (
        2.0 * math.pi / length
    )
    return jnp.concatenate([jnp.cos(angles), jnp.sin(angles)], axis=0).astype(jnp.bfloat16)


def twiddle(row_count, col_count):
    row_index = jnp.arange(row_count, dtype=jnp.int32)[:, None]
    col_index = jnp.arange(col_count, dtype=jnp.int32)[None, :]
    angles = (row_index * col_index % (row_count * col_count)).astype(jnp.float32) * (
        2.0 * math.pi / (row_count * col_count)
    )
    return (jnp.cos(angles), jnp.sin(angles))


def gate_mask(starts, widths, row_count, col_count):
    moment = (
        jnp.arange(row_count, dtype=jnp.int32)[:, None] * col_count
        + jnp.arange(col_count, dtype=jnp.int32)[None, :]
    )
    flags = jnp.zeros((row_count, col_count), dtype=jnp.bool_)
    for number in range(starts.shape[0]):
        flags = flags | (moment >= starts[number]) & (moment < starts[number] + widths[number])
    return flags


def filter_power(template, series, flags, first_table, second_table, twiddle_cos, twiddle_sin):
    count_a = template.shape[1]
    count_b = template.shape[2]
    out_rows = second_table.shape[0] // 2
    tmpl_re = template[0].astype(jnp.float32)
    tmpl_im = template[1].astype(jnp.float32)
    data_re = series[0].astype(jnp.float32)
    data_im = series[1].astype(jnp.float32)
    prod_re = data_re * tmpl_re + data_im * tmpl_im
    prod_im = data_im * tmpl_re - data_re * tmpl_im
    joined = jnp.concatenate([prod_re, prod_im], axis=1).astype(jnp.bfloat16)
    section_one = jnp.dot(first_table, joined, preferred_element_type=jnp.float32)
    section_re = section_one[:count_a, :count_b] - section_one[count_a:, count_b:]
    section_im = section_one[:count_a, count_b:] + section_one[count_a:, :count_b]
    turned = jnp.concatenate(
        [
            section_re * twiddle_cos - section_im * twiddle_sin,
            section_re * twiddle_sin + section_im * twiddle_cos,
        ],
        axis=0,
    ).astype(jnp.bfloat16)
    section_two = lax.dot_general(
        second_table, turned, (((1,), (1,)), ((), ())), preferred_element_type=jnp.float32
    )
    snr_re = section_two[:out_rows, :count_a] - section_two[out_rows:, count_a:]
    snr_im = section_two[:out_rows, count_a:] + section_two[out_rows:, :count_a]
    norm_sq = jnp.sum(tmpl_re * tmpl_re + tmpl_im * tmpl_im) + 1e-06
    snr_power = (snr_re * snr_re + snr_im * snr_im) / norm_sq
    return jnp.where(flags, 0.0, snr_power).astype(jnp.bfloat16)


def series_power(template_re, template_im, series_ref, first, second, turn_cos, turn_sin, starts, widths, row0):
    count_a = template_re.shape[0]
    out_rows = second.shape[0] // 2
    data_re = series_ref[0].astype(jnp.float32)
    data_im = series_ref[1].astype(jnp.float32)
    prod_re = (data_re * template_re + data_im * template_im).astype(jnp.bfloat16)
    prod_im = (data_im * template_re - data_re * template_im).astype(jnp.bfloat16)
    left = jnp.dot(first, prod_re, preferred_element_type=jnp.float32)
    right = jnp.dot(first, prod_im, preferred_element_type=jnp.float32)
    section_re = left[:count_a] - right[count_a:]
    section_im = right[:count_a] + left[count_a:]
    turned_re = (section_re * turn_cos - section_im * turn_sin).astype(jnp.bfloat16)
    turned_im = (section_re * turn_sin + section_im * turn_cos).astype(jnp.bfloat16)
    contract = (((1,), (1,)), ((), ()))
    left = lax.dot_general(second, turned_re, contract, preferred_element_type=jnp.float32)
    right = lax.dot_general(second, turned_im, contract, preferred_element_type=jnp.float32)
    snr_re = left[:out_rows] - right[out_rows:]
    snr_im = right[:out_rows] + left[out_rows:]
    norm_sq = jnp.sum(template_re * template_re + template_im * template_im) + 1e-06
    snr_power = (snr_re * snr_re + snr_im * snr_im) / norm_sq
    moment = (
        lax.broadcasted_iota(jnp.int32, snr_power.shape, 0) + row0
    ) * count_a + lax.broadcasted_iota(jnp.int32, snr_power.shape, 1)
    flags = jnp.zeros(snr_power.shape, dtype=jnp.bool_)
    for number in range(starts.shape[0]):
        begin = starts[number]
        flags = flags | (moment >= begin) & (moment < begin + widths[number])
    return jnp.where(flags, 0.0, snr_power).astype(jnp.bfloat16)


def network_kernel(
    template_ref,
    mine_ref,
    partner_ref,
    first_ref,
    second_ref,
    cos_ref,
    sin_ref,
    mine_start_ref,
    mine_width_ref,
    partner_start_ref,
    partner_width_ref,
    row_ref,
    out_ref,
):
    template_re = template_ref[0].astype(jnp.float32)
    template_im = template_ref[1].astype(jnp.float32)
    first = first_ref[...]
    second = second_ref[...]
    turn_cos = cos_ref[...]
    turn_sin = sin_ref[...]
    row0 = row_ref[0]
    powers = [
        series_power(
            template_re, template_im, series, first, second, turn_cos, turn_sin, starts, widths, row0
        )
        for series, starts, widths in (
            (mine_ref, mine_start_ref, mine_width_ref),
            (partner_ref, partner_start_ref, partner_width_ref),
        )
    ]
    total = powers[0].astype(jnp.float32) + powers[1].astype(jnp.float32)
    out_ref[...] = jnp.sqrt(total).astype(jnp.bfloat16)


def network_call(template, mine, partner, first_table, second_half, twiddle_cos, twiddle_sin, gates, row0):
    vmem = pltpu.MemorySpace.VMEM
    smem = pltpu.MemorySpace.SMEM
    rows = second_half.shape[0] // 2
    return pl.pallas_call(
        network_kernel,
        out_shape=jax.ShapeDtypeStruct((rows, template.shape[1]), jnp.bfloat16),
        in_specs=[pl.BlockSpec(memory_space=vmem)] * 7 + [pl.BlockSpec(memory_space=smem)] * 5,
        out_specs=pl.BlockSpec(memory_space=vmem),
        compiler_params=pltpu.CompilerParams(vmem_limit_bytes=48 * 1024 * 1024),
    )(template, mine, partner, first_table, second_half, twiddle_cos, twiddle_sin, *gates, row0)


def per_device(strain, bank, owners, gate_start, gate_width):
    count_a = strain.shape[2]
    count_b = strain.shape[3]
    block_count = owners.shape[1]
    half_rows = count_b // 2
    first_table = dft_table(count_a)
    second_table = dft_table(count_b)
    twiddle_cos, twiddle_sin = twiddle(count_a, count_b)
    first_table, second_table, twiddle_cos, twiddle_sin = lax.optimization_barrier(
        (first_table, second_table, twiddle_cos, twiddle_sin)
    )
    series = strain[0]
    stored = bank[0]
    detector_side = lax.axis_index("z") % 2
    row_start = detector_side * half_rows
    partner_start, partner_width = [
        from_partner(block, "z", 0) for block in (gate_start[0], gate_width[0])
    ]
    gates = (gate_start[0], gate_width[0], partner_start, partner_width)
    second_half = jnp.concatenate(
        [
            lax.dynamic_slice_in_dim(second_table, row_start, half_rows, 0),
            lax.dynamic_slice_in_dim(second_table, count_b + row_start, half_rows, 0),
        ]
    )
    row0 = jnp.reshape(row_start, (1,)).astype(jnp.int32)
    own_tmpl, other_tmpl, side, partner_series, gates = spread(
        stored, owners[0], "xlo", "z", series, gates
    )
    networks = []
    for template in (own_tmpl, other_tmpl):
        if networks:
            template, _ = lax.optimization_barrier((template, networks[-1]))
        networks.append(
            network_call(
                template,
                series,
                partner_series,
                first_table,
                second_half,
                twiddle_cos,
                twiddle_sin,
                gates,
                row0,
            )
        )
    loudest = butterfly_max(jnp.maximum(networks[0], networks[1]), "tmpl")
    network = jnp.where(
        side == 0, jnp.stack([networks[0], networks[1]]), jnp.stack([networks[1], networks[0]])
    )
    network = network.reshape(block_count, 1, half_rows * count_a)
    loudest = loudest.reshape(1, half_rows * count_a)
    return (network, loudest)


def solution(mesh):
    tmpl_count = mesh.shape["tmpl"]
    seg_count = mesh.shape["seg"]
    grid = Mesh(mesh.devices.reshape(tmpl_count, 2, seg_count // 2), ("tmpl", "xlo", "z"))
    seg = ("xlo", "z")
    in_specs = (
        P(seg, None, None, None),
        P(("tmpl",) + seg, None, None, None),
        P("tmpl", None),
        P(seg, None),
        P(seg, None),
    )
    out_specs = (P("tmpl", seg, None), P(seg, None))
    return jax.shard_map(
        per_device, mesh=grid, in_specs=in_specs, out_specs=out_specs, check_vma=False
    )
```

```python
import math

import jax
import jax.numpy as jnp
from jax import lax
from jax.experimental import pallas as pl
from jax.experimental.pallas import tpu as pltpu
from jax.sharding import Mesh
from jax.sharding import PartitionSpec as P


def spread(stored, owners, row_axis, ring_axis):
    ring = lax.axis_size(ring_axis)
    row = lax.axis_index(row_axis)
    spot = lax.axis_index(ring_axis)
    width = stored.shape[-1]
    chunks = stored.reshape(ring, -1, width)
    bits = ring.bit_length() - 1
    order = [sum(((place >> bit) & 1) << (bits - 1 - bit) for bit in range(bits)) for place in range(ring)]
    outgoing = chunks[jnp.array(order)].reshape(-1, width)
    incoming = lax.all_to_all(outgoing, ring_axis, 0, 0, tiled=True).reshape(ring, -1, width)
    own_holder = jnp.where(row == 0, owners[0], owners[1])
    other_holder = jnp.where(row == 0, owners[1], owners[0])
    mine = lax.dynamic_index_in_dim(incoming, own_holder % ring, 0, keepdims=False)
    theirs = lax.dynamic_index_in_dim(incoming, other_holder % ring, 0, keepdims=False)
    swap = [(0, 1), (1, 0)]
    got = lax.ppermute(theirs, row_axis, swap)
    flat = jnp.where(own_holder // ring == row, mine, got)
    apart = ring // 2
    while apart >= 1:
        side = (spot // apart) % 2
        route = [(low, low ^ apart) for low in range(ring)]
        if apart == 1:
            early = lax.ppermute(flat, row_axis, swap)
        other = lax.ppermute(flat, ring_axis, route)
        if apart == 1:
            late = lax.ppermute(other, row_axis, swap)
            turn = jnp.reshape(side, (1,)).astype(jnp.int32)
            return (flat, other), (early, late), turn, row
        flat = jnp.where(
            side == 0,
            jnp.concatenate([flat, other], axis=0),
            jnp.concatenate([other, flat], axis=0),
        )
        apart //= 2


def butterfly_max(block, axis):
    count = lax.axis_size(axis)
    apart = count // 2
    while apart >= 1:
        route = [(low, low ^ apart) for low in range(count)]
        block = jnp.maximum(block, lax.ppermute(block, axis, route))
        apart //= 2
    return block


def from_partner(block, axis, apart):
    count = lax.axis_size(axis)
    route = []
    for low in range(count):
        high = low | 1 << apart
        if high != low and high < count:
            route += [(low, high), (high, low)]
    return lax.ppermute(block, axis, route)


def dft_table(length):
    positions = jnp.arange(length, dtype=jnp.int32)
    angles = (positions[:, None] * positions[None, :] % length).astype(jnp.float32) * (
        2.0 * math.pi / length
    )
    return jnp.concatenate([jnp.cos(angles), jnp.sin(angles)], axis=0).astype(jnp.bfloat16)


def twiddle(row_count, col_count):
    row_index = jnp.arange(row_count, dtype=jnp.int32)[:, None]
    col_index = jnp.arange(col_count, dtype=jnp.int32)[None, :]
    angles = (row_index * col_index % (row_count * col_count)).astype(jnp.float32) * (
        2.0 * math.pi / (row_count * col_count)
    )
    return (jnp.cos(angles), jnp.sin(angles))


def gate_mask(starts, widths, row_count, col_count):
    moment = (
        jnp.arange(row_count, dtype=jnp.int32)[:, None] * col_count
        + jnp.arange(col_count, dtype=jnp.int32)[None, :]
    )
    flags = jnp.zeros((row_count, col_count), dtype=jnp.bool_)
    for number in range(starts.shape[0]):
        flags = flags | (moment >= starts[number]) & (moment < starts[number] + widths[number])
    return flags


def filter_power(template, series, flags, first_table, second_table, twiddle_cos, twiddle_sin):
    count_a = template.shape[1]
    count_b = template.shape[2]
    out_rows = second_table.shape[0] // 2
    tmpl_re = template[0].astype(jnp.float32)
    tmpl_im = template[1].astype(jnp.float32)
    data_re = series[0].astype(jnp.float32)
    data_im = series[1].astype(jnp.float32)
    prod_re = data_re * tmpl_re + data_im * tmpl_im
    prod_im = data_im * tmpl_re - data_re * tmpl_im
    joined = jnp.concatenate([prod_re, prod_im], axis=1).astype(jnp.bfloat16)
    section_one = jnp.dot(first_table, joined, preferred_element_type=jnp.float32)
    section_re = section_one[:count_a, :count_b] - section_one[count_a:, count_b:]
    section_im = section_one[:count_a, count_b:] + section_one[count_a:, :count_b]
    turned = jnp.concatenate(
        [
            section_re * twiddle_cos - section_im * twiddle_sin,
            section_re * twiddle_sin + section_im * twiddle_cos,
        ],
        axis=0,
    ).astype(jnp.bfloat16)
    section_two = lax.dot_general(
        second_table, turned, (((1,), (1,)), ((), ())), preferred_element_type=jnp.float32
    )
    snr_re = section_two[:out_rows, :count_a] - section_two[out_rows:, count_a:]
    snr_im = section_two[:out_rows, count_a:] + section_two[out_rows:, :count_a]
    norm_sq = jnp.sum(tmpl_re * tmpl_re + tmpl_im * tmpl_im) + 1e-06
    snr_power = (snr_re * snr_re + snr_im * snr_im) / norm_sq
    return jnp.where(flags, 0.0, snr_power).astype(jnp.bfloat16)


def filter_kernel(
    low_ref, high_ref, swap_ref, series_ref, first_ref, second_ref, cos_ref, sin_ref, start_ref, width_ref, out_ref
):
    count_a = low_ref.shape[0]
    out_rows = second_ref.shape[0] // 2
    swap = swap_ref[0] == 1
    low = low_ref[...].astype(jnp.float32)
    high = high_ref[...].astype(jnp.float32)
    tmpl_re = jnp.where(swap, high, low)
    tmpl_im = jnp.where(swap, low, high)
    data_re = series_ref[0].astype(jnp.float32)
    data_im = series_ref[1].astype(jnp.float32)
    prod_re = (data_re * tmpl_re + data_im * tmpl_im).astype(jnp.bfloat16)
    prod_im = (data_im * tmpl_re - data_re * tmpl_im).astype(jnp.bfloat16)
    first = first_ref[...]
    left = jnp.dot(first, prod_re, preferred_element_type=jnp.float32)
    right = jnp.dot(first, prod_im, preferred_element_type=jnp.float32)
    section_re = left[:count_a] - right[count_a:]
    section_im = right[:count_a] + left[count_a:]
    turn_cos = cos_ref[...]
    turn_sin = sin_ref[...]
    turned_re = (section_re * turn_cos - section_im * turn_sin).astype(jnp.bfloat16)
    turned_im = (section_re * turn_sin + section_im * turn_cos).astype(jnp.bfloat16)
    second = second_ref[...]
    contract = (((1,), (1,)), ((), ()))
    left = lax.dot_general(second, turned_re, contract, preferred_element_type=jnp.float32)
    right = lax.dot_general(second, turned_im, contract, preferred_element_type=jnp.float32)
    snr_re = left[:out_rows] - right[out_rows:]
    snr_im = right[:out_rows] + left[out_rows:]
    norm_sq = jnp.sum(tmpl_re * tmpl_re + tmpl_im * tmpl_im) + 1e-06
    snr_power = (snr_re * snr_re + snr_im * snr_im) / norm_sq
    moment = (
        lax.broadcasted_iota(jnp.int32, snr_power.shape, 0) * count_a
        + lax.broadcasted_iota(jnp.int32, snr_power.shape, 1)
    )
    flags = jnp.zeros(snr_power.shape, dtype=jnp.bool_)
    for number in range(start_ref.shape[0]):
        begin = start_ref[number]
        flags = flags | (moment >= begin) & (moment < begin + width_ref[number])
    out_ref[...] = jnp.where(flags, 0.0, snr_power).astype(jnp.bfloat16)


def filter_call(halves, swap, series, first_table, second_table, twiddle_cos, twiddle_sin, starts, widths):
    vmem = pltpu.MemorySpace.VMEM
    smem = pltpu.MemorySpace.SMEM
    rows = second_table.shape[0] // 2
    specs = [pl.BlockSpec(memory_space=vmem)] * 2 + [pl.BlockSpec(memory_space=smem)]
    specs += [pl.BlockSpec(memory_space=vmem)] * 5 + [pl.BlockSpec(memory_space=smem)] * 2
    return pl.pallas_call(
        filter_kernel,
        out_shape=jax.ShapeDtypeStruct((rows, halves[0].shape[1]), jnp.bfloat16),
        in_specs=specs,
        out_specs=pl.BlockSpec(memory_space=vmem),
        compiler_params=pltpu.CompilerParams(vmem_limit_bytes=48 * 1024 * 1024),
    )(*halves, swap, series, first_table, second_table, twiddle_cos, twiddle_sin, starts, widths)


def per_device(strain, bank, owners, gate_start, gate_width):
    count_a = strain.shape[2]
    count_b = strain.shape[3]
    block_count = owners.shape[1]
    half_rows = count_b // 2
    first_table = dft_table(count_a)
    second_table = dft_table(count_b)
    twiddle_cos, twiddle_sin = twiddle(count_a, count_b)
    first_table, second_table, twiddle_cos, twiddle_sin = lax.optimization_barrier(
        (first_table, second_table, twiddle_cos, twiddle_sin)
    )
    series = strain[0]
    stored = bank[0]
    detector_side = lax.axis_index("z") % 2
    row_start = detector_side * half_rows
    own_tmpl, other_tmpl, turn, side = spread(stored, owners[0], "xlo", "z")
    networks = []
    power = None
    for template in (own_tmpl, other_tmpl):
        if power is not None:
            template, power = lax.optimization_barrier((template, power))
        power = filter_call(
            template,
            turn,
            series,
            first_table,
            second_table,
            twiddle_cos,
            twiddle_sin,
            gate_start[0],
            gate_width[0],
        )
        own_half = lax.dynamic_slice_in_dim(power, row_start, half_rows, 0)
        other_half = lax.dynamic_slice_in_dim(power, half_rows - row_start, half_rows, 0)
        partner = from_partner(other_half, "z", 0)
        networks.append(
            jnp.sqrt(own_half.astype(jnp.float32) + partner.astype(jnp.float32)).astype(
                jnp.bfloat16
            )
        )
    loudest = butterfly_max(jnp.maximum(networks[0], networks[1]), "tmpl")
    network = jnp.where(
        side == 0, jnp.stack([networks[0], networks[1]]), jnp.stack([networks[1], networks[0]])
    )
    network = network.reshape(block_count, 1, half_rows * count_a)
    loudest = loudest.reshape(1, half_rows * count_a)
    return (network, loudest)


def solution(mesh):
    tmpl_count = mesh.shape["tmpl"]
    seg_count = mesh.shape["seg"]
    grid = Mesh(mesh.devices.reshape(tmpl_count, 2, seg_count // 2), ("tmpl", "xlo", "z"))
    seg = ("xlo", "z")
    in_specs = (
        P(seg, None, None, None),
        P(("tmpl",) + seg, None, None, None),
        P("tmpl", None),
        P(seg, None),
        P(seg, None),
    )
    out_specs = (P("tmpl", seg, None), P(seg, None))
    return jax.shard_map(
        per_device, mesh=grid, in_specs=in_specs, out_specs=out_specs, check_vma=False
    )
```

```python
import math

import jax
import jax.numpy as jnp
from jax import lax
from jax.experimental import pallas as pl
from jax.experimental.pallas import tpu as pltpu
from jax.sharding import Mesh
from jax.sharding import PartitionSpec as P


def spread(stored, owners, row_axis, ring_axis):
    ring = lax.axis_size(ring_axis)
    row = lax.axis_index(row_axis)
    spot = lax.axis_index(ring_axis)
    width = stored.shape[-1]
    chunks = stored.reshape(ring, -1, width)
    bits = ring.bit_length() - 1
    order = [sum(((place >> bit) & 1) << (bits - 1 - bit) for bit in range(bits)) for place in range(ring)]
    outgoing = chunks[jnp.array(order)].reshape(-1, width)
    incoming = lax.all_to_all(outgoing, ring_axis, 0, 0, tiled=True).reshape(ring, -1, width)
    own_holder = jnp.where(row == 0, owners[0], owners[1])
    other_holder = jnp.where(row == 0, owners[1], owners[0])
    mine = lax.dynamic_index_in_dim(incoming, own_holder % ring, 0, keepdims=False)
    theirs = lax.dynamic_index_in_dim(incoming, other_holder % ring, 0, keepdims=False)
    swap = [(0, 1), (1, 0)]
    got = lax.ppermute(theirs, row_axis, swap)
    flat = jnp.where(own_holder // ring == row, mine, got)
    apart = ring // 2
    while apart >= 1:
        side = (spot // apart) % 2
        route = [(low, low ^ apart) for low in range(ring)]
        if apart == 1:
            early = lax.ppermute(flat, row_axis, swap)
        other = lax.ppermute(flat, ring_axis, route)
        if apart == 1:
            late = lax.ppermute(other, row_axis, swap)
            theirs = jnp.where(
                side == 0,
                jnp.concatenate([early, late], axis=0),
                jnp.concatenate([late, early], axis=0),
            )
        flat = jnp.where(
            side == 0,
            jnp.concatenate([flat, other], axis=0),
            jnp.concatenate([other, flat], axis=0),
        )
        apart //= 2
    return flat.reshape(stored.shape), theirs.reshape(stored.shape), row


def butterfly_max(block, axis):
    count = lax.axis_size(axis)
    apart = count // 2
    while apart >= 1:
        route = [(low, low ^ apart) for low in range(count)]
        block = jnp.maximum(block, lax.ppermute(block, axis, route))
        apart //= 2
    return block


def from_partner(block, axis, apart):
    count = lax.axis_size(axis)
    route = []
    for low in range(count):
        high = low | 1 << apart
        if high != low and high < count:
            route += [(low, high), (high, low)]
    return lax.ppermute(block, axis, route)


def dft_table(length):
    positions = jnp.arange(length, dtype=jnp.int32)
    angles = (positions[:, None] * positions[None, :] % length).astype(jnp.float32) * (
        2.0 * math.pi / length
    )
    return jnp.concatenate([jnp.cos(angles), jnp.sin(angles)], axis=0).astype(jnp.bfloat16)


def twiddle(row_count, col_count):
    row_index = jnp.arange(row_count, dtype=jnp.int32)[:, None]
    col_index = jnp.arange(col_count, dtype=jnp.int32)[None, :]
    angles = (row_index * col_index % (row_count * col_count)).astype(jnp.float32) * (
        2.0 * math.pi / (row_count * col_count)
    )
    return (jnp.cos(angles), jnp.sin(angles))


def gate_mask(starts, widths, row_count, col_count):
    moment = (
        jnp.arange(row_count, dtype=jnp.int32)[:, None] * col_count
        + jnp.arange(col_count, dtype=jnp.int32)[None, :]
    )
    flags = jnp.zeros((row_count, col_count), dtype=jnp.bool_)
    for number in range(starts.shape[0]):
        flags = flags | (moment >= starts[number]) & (moment < starts[number] + widths[number])
    return flags


def filter_power(template, series, flags, first_table, second_table, twiddle_cos, twiddle_sin):
    count_a = template.shape[1]
    count_b = template.shape[2]
    out_rows = second_table.shape[0] // 2
    tmpl_re = template[0].astype(jnp.float32)
    tmpl_im = template[1].astype(jnp.float32)
    data_re = series[0].astype(jnp.float32)
    data_im = series[1].astype(jnp.float32)
    prod_re = data_re * tmpl_re + data_im * tmpl_im
    prod_im = data_im * tmpl_re - data_re * tmpl_im
    joined = jnp.concatenate([prod_re, prod_im], axis=1).astype(jnp.bfloat16)
    section_one = jnp.dot(first_table, joined, preferred_element_type=jnp.float32)
    section_re = section_one[:count_a, :count_b] - section_one[count_a:, count_b:]
    section_im = section_one[:count_a, count_b:] + section_one[count_a:, :count_b]
    turned = jnp.concatenate(
        [
            section_re * twiddle_cos - section_im * twiddle_sin,
            section_re * twiddle_sin + section_im * twiddle_cos,
        ],
        axis=0,
    ).astype(jnp.bfloat16)
    section_two = lax.dot_general(
        second_table, turned, (((1,), (1,)), ((), ())), preferred_element_type=jnp.float32
    )
    snr_re = section_two[:out_rows, :count_a] - section_two[out_rows:, count_a:]
    snr_im = section_two[:out_rows, count_a:] + section_two[out_rows:, :count_a]
    norm_sq = jnp.sum(tmpl_re * tmpl_re + tmpl_im * tmpl_im) + 1e-06
    snr_power = (snr_re * snr_re + snr_im * snr_im) / norm_sq
    return jnp.where(flags, 0.0, snr_power).astype(jnp.bfloat16)


def filter_kernel(
    template_ref, series_ref, first_ref, second_ref, cos_ref, sin_ref, start_ref, width_ref, out_ref
):
    count_a = template_ref.shape[1]
    count_b = template_ref.shape[2]
    out_rows = second_ref.shape[0] // 2
    tmpl_re = template_ref[0].astype(jnp.float32)
    tmpl_im = template_ref[1].astype(jnp.float32)
    data_re = series_ref[0].astype(jnp.float32)
    data_im = series_ref[1].astype(jnp.float32)
    prod_re = (data_re * tmpl_re + data_im * tmpl_im).astype(jnp.bfloat16)
    prod_im = (data_im * tmpl_re - data_re * tmpl_im).astype(jnp.bfloat16)
    first = first_ref[...]
    left = jnp.dot(first, prod_re, preferred_element_type=jnp.float32)
    right = jnp.dot(first, prod_im, preferred_element_type=jnp.float32)
    section_re = left[:count_a] - right[count_a:]
    section_im = right[:count_a] + left[count_a:]
    turn_cos = cos_ref[...]
    turn_sin = sin_ref[...]
    turned_re = (section_re * turn_cos - section_im * turn_sin).astype(jnp.bfloat16)
    turned_im = (section_re * turn_sin + section_im * turn_cos).astype(jnp.bfloat16)
    second = second_ref[...]
    contract = (((1,), (1,)), ((), ()))
    left = lax.dot_general(second, turned_re, contract, preferred_element_type=jnp.float32)
    right = lax.dot_general(second, turned_im, contract, preferred_element_type=jnp.float32)
    snr_re = left[:out_rows] - right[out_rows:]
    snr_im = right[:out_rows] + left[out_rows:]
    norm_sq = jnp.sum(tmpl_re * tmpl_re + tmpl_im * tmpl_im) + 1e-06
    snr_power = (snr_re * snr_re + snr_im * snr_im) / norm_sq
    moment = (
        lax.broadcasted_iota(jnp.int32, snr_power.shape, 0) * count_a
        + lax.broadcasted_iota(jnp.int32, snr_power.shape, 1)
    )
    flags = jnp.zeros(snr_power.shape, dtype=jnp.bool_)
    for number in range(start_ref.shape[0]):
        begin = start_ref[number]
        flags = flags | (moment >= begin) & (moment < begin + width_ref[number])
    out_ref[...] = jnp.where(flags, 0.0, snr_power).astype(jnp.bfloat16)


def filter_call(template, series, first_table, second_table, twiddle_cos, twiddle_sin, starts, widths):
    vmem = pltpu.MemorySpace.VMEM
    smem = pltpu.MemorySpace.SMEM
    rows = second_table.shape[0] // 2
    return pl.pallas_call(
        filter_kernel,
        out_shape=jax.ShapeDtypeStruct((rows, template.shape[1]), jnp.bfloat16),
        in_specs=[pl.BlockSpec(memory_space=vmem)] * 6 + [pl.BlockSpec(memory_space=smem)] * 2,
        out_specs=pl.BlockSpec(memory_space=vmem),
        compiler_params=pltpu.CompilerParams(vmem_limit_bytes=48 * 1024 * 1024),
    )(template, series, first_table, second_table, twiddle_cos, twiddle_sin, starts, widths)


def per_device(strain, bank, owners, gate_start, gate_width):
    count_a = strain.shape[2]
    count_b = strain.shape[3]
    block_count = owners.shape[1]
    half_rows = count_b // 2
    first_table = dft_table(count_a)
    second_table = dft_table(count_b)
    twiddle_cos, twiddle_sin = twiddle(count_a, count_b)
    first_table, second_table, twiddle_cos, twiddle_sin = lax.optimization_barrier(
        (first_table, second_table, twiddle_cos, twiddle_sin)
    )
    series = strain[0]
    stored = bank[0]
    detector_side = lax.axis_index("z") % 2
    row_start = detector_side * half_rows
    own_tmpl, other_tmpl, side = spread(stored, owners[0], "xlo", "z")
    powers = []
    for template in (own_tmpl, other_tmpl):
        if powers:
            template, _ = lax.optimization_barrier((template, powers[-1]))
        powers.append(
            filter_call(
                template,
                series,
                first_table,
                second_table,
                twiddle_cos,
                twiddle_sin,
                gate_start[0],
                gate_width[0],
            )
        )
    stacked = jnp.stack(powers)
    own_half = lax.dynamic_slice_in_dim(stacked, row_start, half_rows, 1)
    other_half = lax.dynamic_slice_in_dim(stacked, half_rows - row_start, half_rows, 1)
    partner = from_partner(other_half, "z", 0)
    both = jnp.sqrt(own_half.astype(jnp.float32) + partner.astype(jnp.float32)).astype(jnp.bfloat16)
    networks = [both[0], both[1]]
    loudest = butterfly_max(jnp.maximum(networks[0], networks[1]), "tmpl")
    network = jnp.where(
        side == 0, jnp.stack([networks[0], networks[1]]), jnp.stack([networks[1], networks[0]])
    )
    network = network.reshape(block_count, 1, half_rows * count_a)
    loudest = loudest.reshape(1, half_rows * count_a)
    return (network, loudest)


def solution(mesh):
    tmpl_count = mesh.shape["tmpl"]
    seg_count = mesh.shape["seg"]
    grid = Mesh(mesh.devices.reshape(tmpl_count, 2, seg_count // 2), ("tmpl", "xlo", "z"))
    seg = ("xlo", "z")
    in_specs = (
        P(seg, None, None, None),
        P(("tmpl",) + seg, None, None, None),
        P("tmpl", None),
        P(seg, None),
        P(seg, None),
    )
    out_specs = (P("tmpl", seg, None), P(seg, None))
    return jax.shard_map(
        per_device, mesh=grid, in_specs=in_specs, out_specs=out_specs, check_vma=False
    )
```

```python
import math

import jax
import jax.numpy as jnp
from jax import lax
from jax.experimental import pallas as pl
from jax.experimental.pallas import tpu as pltpu
from jax.sharding import Mesh
from jax.sharding import PartitionSpec as P


def spread(stored, owners, row_axis, ring_axis):
    ring = lax.axis_size(ring_axis)
    row = lax.axis_index(row_axis)
    spot = lax.axis_index(ring_axis)
    width = stored.shape[-1]
    chunks = stored.reshape(ring, -1, width)
    bits = ring.bit_length() - 1
    order = [sum(((place >> bit) & 1) << (bits - 1 - bit) for bit in range(bits)) for place in range(ring)]
    outgoing = chunks[jnp.array(order)].reshape(-1, width)
    incoming = lax.all_to_all(outgoing, ring_axis, 0, 0, tiled=True).reshape(ring, -1, width)
    own_holder = jnp.where(row == 0, owners[0], owners[1])
    other_holder = jnp.where(row == 0, owners[1], owners[0])
    mine = lax.dynamic_index_in_dim(incoming, own_holder % ring, 0, keepdims=False)
    theirs = lax.dynamic_index_in_dim(incoming, other_holder % ring, 0, keepdims=False)
    swap = [(0, 1), (1, 0)]
    got = lax.ppermute(theirs, row_axis, swap)
    flat = jnp.where(own_holder // ring == row, mine, got)
    apart = ring // 2
    while apart >= 1:
        side = (spot // apart) % 2
        route = [(low, low ^ apart) for low in range(ring)]
        if apart == 1:
            early = lax.ppermute(flat, row_axis, swap)
        other = lax.ppermute(flat, ring_axis, route)
        if apart == 1:
            late = lax.ppermute(other, row_axis, swap)
            theirs = jnp.where(
                side == 0,
                jnp.concatenate([early, late], axis=0),
                jnp.concatenate([late, early], axis=0),
            )
        flat = jnp.where(
            side == 0,
            jnp.concatenate([flat, other], axis=0),
            jnp.concatenate([other, flat], axis=0),
        )
        apart //= 2
    return flat.reshape(stored.shape), theirs.reshape(stored.shape), row


def butterfly_max(block, axis, rider):
    count = lax.axis_size(axis)
    apart = count // 2
    while apart >= 1:
        route = [(low, low ^ apart) for low in range(count)]
        block = jnp.maximum(block, lax.ppermute(block, axis, route))
        if apart == count // 2:
            block, rider = lax.optimization_barrier((block, rider))
        apart //= 2
    return block, rider


def from_partner(block, axis, apart):
    count = lax.axis_size(axis)
    route = []
    for low in range(count):
        high = low | 1 << apart
        if high != low and high < count:
            route += [(low, high), (high, low)]
    return lax.ppermute(block, axis, route)


def dft_table(length):
    positions = jnp.arange(length, dtype=jnp.int32)
    angles = (positions[:, None] * positions[None, :] % length).astype(jnp.float32) * (
        2.0 * math.pi / length
    )
    return jnp.concatenate([jnp.cos(angles), jnp.sin(angles)], axis=0).astype(jnp.bfloat16)


def twiddle(row_count, col_count):
    row_index = jnp.arange(row_count, dtype=jnp.int32)[:, None]
    col_index = jnp.arange(col_count, dtype=jnp.int32)[None, :]
    angles = (row_index * col_index % (row_count * col_count)).astype(jnp.float32) * (
        2.0 * math.pi / (row_count * col_count)
    )
    return (jnp.cos(angles), jnp.sin(angles))


def gate_mask(starts, widths, row_count, col_count):
    moment = (
        jnp.arange(row_count, dtype=jnp.int32)[:, None] * col_count
        + jnp.arange(col_count, dtype=jnp.int32)[None, :]
    )
    flags = jnp.zeros((row_count, col_count), dtype=jnp.bool_)
    for number in range(starts.shape[0]):
        flags = flags | (moment >= starts[number]) & (moment < starts[number] + widths[number])
    return flags


def filter_power(template, series, flags, first_table, second_table, twiddle_cos, twiddle_sin):
    count_a = template.shape[1]
    count_b = template.shape[2]
    out_rows = second_table.shape[0] // 2
    tmpl_re = template[0].astype(jnp.float32)
    tmpl_im = template[1].astype(jnp.float32)
    data_re = series[0].astype(jnp.float32)
    data_im = series[1].astype(jnp.float32)
    prod_re = data_re * tmpl_re + data_im * tmpl_im
    prod_im = data_im * tmpl_re - data_re * tmpl_im
    joined = jnp.concatenate([prod_re, prod_im], axis=1).astype(jnp.bfloat16)
    section_one = jnp.dot(first_table, joined, preferred_element_type=jnp.float32)
    section_re = section_one[:count_a, :count_b] - section_one[count_a:, count_b:]
    section_im = section_one[:count_a, count_b:] + section_one[count_a:, :count_b]
    turned = jnp.concatenate(
        [
            section_re * twiddle_cos - section_im * twiddle_sin,
            section_re * twiddle_sin + section_im * twiddle_cos,
        ],
        axis=0,
    ).astype(jnp.bfloat16)
    section_two = lax.dot_general(
        second_table, turned, (((1,), (1,)), ((), ())), preferred_element_type=jnp.float32
    )
    snr_re = section_two[:out_rows, :count_a] - section_two[out_rows:, count_a:]
    snr_im = section_two[:out_rows, count_a:] + section_two[out_rows:, :count_a]
    norm_sq = jnp.sum(tmpl_re * tmpl_re + tmpl_im * tmpl_im) + 1e-06
    snr_power = (snr_re * snr_re + snr_im * snr_im) / norm_sq
    return jnp.where(flags, 0.0, snr_power).astype(jnp.bfloat16)


def filter_kernel(
    template_ref, series_ref, first_ref, second_ref, cos_ref, sin_ref, start_ref, width_ref, out_ref
):
    count_a = template_ref.shape[1]
    count_b = template_ref.shape[2]
    out_rows = second_ref.shape[0] // 2
    tmpl_re = template_ref[0].astype(jnp.float32)
    tmpl_im = template_ref[1].astype(jnp.float32)
    data_re = series_ref[0].astype(jnp.float32)
    data_im = series_ref[1].astype(jnp.float32)
    prod_re = (data_re * tmpl_re + data_im * tmpl_im).astype(jnp.bfloat16)
    prod_im = (data_im * tmpl_re - data_re * tmpl_im).astype(jnp.bfloat16)
    first = first_ref[...]
    left = jnp.dot(first, prod_re, preferred_element_type=jnp.float32)
    right = jnp.dot(first, prod_im, preferred_element_type=jnp.float32)
    section_re = left[:count_a] - right[count_a:]
    section_im = right[:count_a] + left[count_a:]
    turn_cos = cos_ref[...]
    turn_sin = sin_ref[...]
    turned_re = (section_re * turn_cos - section_im * turn_sin).astype(jnp.bfloat16)
    turned_im = (section_re * turn_sin + section_im * turn_cos).astype(jnp.bfloat16)
    second = second_ref[...]
    contract = (((1,), (1,)), ((), ()))
    left = lax.dot_general(second, turned_re, contract, preferred_element_type=jnp.float32)
    right = lax.dot_general(second, turned_im, contract, preferred_element_type=jnp.float32)
    snr_re = left[:out_rows] - right[out_rows:]
    snr_im = right[:out_rows] + left[out_rows:]
    norm_sq = jnp.sum(tmpl_re * tmpl_re + tmpl_im * tmpl_im) + 1e-06
    snr_power = (snr_re * snr_re + snr_im * snr_im) / norm_sq
    moment = (
        lax.broadcasted_iota(jnp.int32, snr_power.shape, 0) * count_a
        + lax.broadcasted_iota(jnp.int32, snr_power.shape, 1)
    )
    flags = jnp.zeros(snr_power.shape, dtype=jnp.bool_)
    for number in range(start_ref.shape[0]):
        begin = start_ref[number]
        flags = flags | (moment >= begin) & (moment < begin + width_ref[number])
    out_ref[...] = jnp.where(flags, 0.0, snr_power).astype(jnp.bfloat16)


def filter_call(template, series, first_table, second_table, twiddle_cos, twiddle_sin, starts, widths):
    vmem = pltpu.MemorySpace.VMEM
    smem = pltpu.MemorySpace.SMEM
    rows = second_table.shape[0] // 2
    return pl.pallas_call(
        filter_kernel,
        out_shape=jax.ShapeDtypeStruct((rows, template.shape[1]), jnp.bfloat16),
        in_specs=[pl.BlockSpec(memory_space=vmem)] * 6 + [pl.BlockSpec(memory_space=smem)] * 2,
        out_specs=pl.BlockSpec(memory_space=vmem),
        compiler_params=pltpu.CompilerParams(vmem_limit_bytes=48 * 1024 * 1024),
    )(template, series, first_table, second_table, twiddle_cos, twiddle_sin, starts, widths)


def per_device(strain, bank, owners, gate_start, gate_width):
    count_a = strain.shape[2]
    count_b = strain.shape[3]
    block_count = owners.shape[1]
    half_rows = count_b // 2
    first_table = dft_table(count_a)
    second_table = dft_table(count_b)
    twiddle_cos, twiddle_sin = twiddle(count_a, count_b)
    first_table, second_table, twiddle_cos, twiddle_sin = lax.optimization_barrier(
        (first_table, second_table, twiddle_cos, twiddle_sin)
    )
    series = strain[0]
    stored = bank[0]
    detector_side = lax.axis_index("z") % 2
    row_start = detector_side * half_rows
    own_tmpl, other_tmpl, side = spread(stored, owners[0], "xlo", "z")
    networks = []
    power = None
    for template in (own_tmpl, other_tmpl):
        if power is not None:
            template, power = lax.optimization_barrier((template, power))
        power = filter_call(
            template,
            series,
            first_table,
            second_table,
            twiddle_cos,
            twiddle_sin,
            gate_start[0],
            gate_width[0],
        )
        own_half = lax.dynamic_slice_in_dim(power, row_start, half_rows, 0)
        other_half = lax.dynamic_slice_in_dim(power, half_rows - row_start, half_rows, 0)
        partner = from_partner(other_half, "z", 0)
        networks.append(
            jnp.sqrt(own_half.astype(jnp.float32) + partner.astype(jnp.float32)).astype(
                jnp.bfloat16
            )
        )
    network = jnp.where(
        side == 0, jnp.stack([networks[0], networks[1]]), jnp.stack([networks[1], networks[0]])
    )
    loudest, network = butterfly_max(jnp.maximum(networks[0], networks[1]), "tmpl", network)
    network = network.reshape(block_count, 1, half_rows * count_a)
    loudest = loudest.reshape(1, half_rows * count_a)
    return (network, loudest)


def solution(mesh):
    tmpl_count = mesh.shape["tmpl"]
    seg_count = mesh.shape["seg"]
    grid = Mesh(mesh.devices.reshape(tmpl_count, 2, seg_count // 2), ("tmpl", "xlo", "z"))
    seg = ("xlo", "z")
    in_specs = (
        P(seg, None, None, None),
        P(("tmpl",) + seg, None, None, None),
        P("tmpl", None),
        P(seg, None),
        P(seg, None),
    )
    out_specs = (P("tmpl", seg, None), P(seg, None))
    return jax.shard_map(
        per_device, mesh=grid, in_specs=in_specs, out_specs=out_specs, check_vma=False
    )
```
